32 devices in a mesh: tok: 4 (over y, x), exp: 8 (over z, core).
Axes of the slice: x: 2, y: 2, z: 4, core: 2. Of those that a mesh axis runs over, the one named last changes fastest.
Arguments:
- captured: bfloat16 [2048, 8, 1024], P(('tok', 'exp')), may hold values from -16 to 16
- expert_ids: int32 [2048, 8], P(('tok', 'exp')), may hold values from 0 to 31, all different within a row; in each aligned block of 32 rows (0 to 31, 32 to 63, ...) at most 16 rows name the same one
Outputs:
- whitening: float32 [32, 1024, 1024], P(('tok', 'exp'))
The draws below stay inside these ranges and needn't reach their ends.
Inputs may be any that keep to these rules, and one draw needn't show every extreme that they name: `expert_ids`: each row names 8 different experts; every expert is named by some row. In each aligned block of 32 token rows no expert is named more than 16 times, and in some block some expert is named exactly 16 times.
All inputs are finite; a program needn't handle non-finite values.
Results may differ from the reference program's by a relative error of at most 0.0003.
Values may be sent and summed in bfloat16 or wider, within the bound.
A program may use at most 64 MiB of HBM per device.

```python
import math
import jax
import jax.numpy as jnp
import numpy as np
from jax import lax

H = 1024
TOP = 8
TOK_DEV = 64
EXPERTS = 32
TOKENS = 2048
MOST = 16


def draw_captured(key, part):
    subkeys = jax.random.split(key, 3)
    columns = jnp.exp(jax.random.uniform(subkeys[0], (H,), jnp.float32, math.log(0.3), math.log(3.0)))
    row_scale = jnp.exp(jax.random.uniform(subkeys[1], (TOKENS, TOP, 1), jnp.float32, math.log(0.5), math.log(2.0)))
    values = jax.random.normal(subkeys[2], (TOKENS, TOP, H), jnp.float32) * columns * row_scale
    return jnp.clip(values, -16.0, 16.0).astype(jnp.bfloat16)


def deal_out(own_key, own, number, rows, amount, top, limit, lean):
    order = jax.random.permutation(own_key, amount)
    packed, usual = load_shares(amount, rows * top, limit, lean, True), load_shares(amount, rows * top, limit, lean, False)
    places = jnp.arange(amount)

    def named(sizes, turn):
        used = int((sizes > 0).sum())
        fixed = max(1, used // 4)
        shifted = fixed + (places - fixed + turn * (used - fixed)) % max(1, amount - fixed)
        return jnp.zeros((amount,), jnp.int32).at[order[jnp.where(places < fixed, places, shifted)]].set(jnp.asarray(sizes, jnp.int32))

    sizes = jnp.where(number % 4 == 0, named(packed, number // 4), named(usual, number - number // 4 - 1))
    mixed = jax.random.permutation(jax.random.fold_in(own, 3), amount)
    donor, receiver = mixed[0:amount // 2 * 2:2], mixed[1:amount // 2 * 2:2]
    margin = jnp.minimum(sizes[donor] - 1, limit - sizes[receiver]) // 2
    margin = jnp.where((donor == order[0]) | (receiver == order[0]) | (sizes[receiver] == 0), 0, jnp.maximum(margin, 0))
    shifted = jax.random.randint(jax.random.fold_in(own, 4), (amount // 2,), 0, 1 << 20) % (margin + 1)
    sizes = sizes.at[donor].add(-shifted).at[receiver].add(shifted)
    items = jnp.searchsorted(jnp.cumsum(sizes), jnp.arange(rows * top), side="right").astype(jnp.int32)
    table = items.reshape(top, rows).T
    table = table[jax.random.permutation(jax.random.fold_in(own, 1), rows)]
    turn = jax.random.randint(jax.random.fold_in(own, 2), (rows, 1), 0, top)
    return jnp.take_along_axis(table, (jnp.arange(top)[None, :] + turn) % top, axis=1)


def load_shares(number_of, total, reach, skew, full):
    weights = [(1 << 20) // math.isqrt(grade ** skew) + 1 for grade in range(1, number_of + 1)]
    largest = reach if full else min(reach, max(-(-total // number_of), total * weights[0] // sum(weights)))
    least = 1 if total - largest >= number_of - 1 else 0
    given, rest = [largest] + [least] * (number_of - 1), total - largest - least * (number_of - 1)
    while rest > 0:
        movable = [i for i in range(1, number_of) if given[i] < largest] or [i for i in range(1, number_of) if given[i] < reach]
        mass, left = sum([weights[i] for i in movable]), rest
        for i in movable:
            addition = min(reach - given[i], max(1, left * weights[i] // mass), rest)
            given[i] = given[i] + addition
            rest = rest - addition
    return np.array(given)


def setup_inputs(seed: int = 0) -> dict:
    arg_keys = jax.random.split(jax.random.key(seed), 3)
    captured = draw_captured(jax.random.fold_in(arg_keys[2], 71), 0)
    expert_ids_keys = jax.random.split(jax.random.fold_in(arg_keys[1], 1), TOKENS // (TOK_DEV // 2))
    expert_ids_turns = jax.random.permutation(jax.random.fold_in(arg_keys[1], 3), TOKENS // (TOK_DEV // 2))
    expert_ids = jax.vmap(lambda own, number: deal_out(jax.random.fold_in(arg_keys[1], 2), own, number, TOK_DEV // 2, EXPERTS, TOP, MOST, 2))(expert_ids_keys, expert_ids_turns).reshape((TOKENS, TOP))
    return {"captured": captured, "expert_ids": expert_ids}


damping = 0.1

def whiten(gram, count):
    hess = gram / count
    shift = damping * jnp.mean(jnp.diagonal(hess))
    identity = jnp.eye(hess.shape[0], dtype=hess.dtype)
    hess = hess + shift * identity
    factor = jnp.linalg.cholesky(hess)
    return lax.linalg.triangular_solve(factor, identity, left_side=True, lower=True)

def reference(captured, expert_ids):
    flat_rows = captured.reshape(TOKENS * TOP, H)
    flat_ids = expert_ids.reshape(-1).astype(jnp.int32)
    expert_iota = jnp.arange(EXPERTS).astype(jnp.int32)
    counts_int = jnp.sum((flat_ids[:, None] == expert_iota[None, :]).astype(jnp.int32), axis=0).astype(jnp.int32)
    starts = (jnp.cumsum(counts_int) - counts_int).astype(jnp.int32)
    order = jnp.argsort(flat_ids, stable=True)
    capacity = EXPERTS * 2 * MOST
    ordered = jnp.concatenate([flat_rows[order], jnp.zeros((capacity, H), flat_rows.dtype)], axis=0)

    def one_expert(expert):
        start = starts[expert].astype(jnp.int32)
        count = counts_int[expert]
        block = lax.dynamic_slice_in_dim(ordered, start, capacity, 0)
        keep = jnp.arange(capacity).astype(jnp.int32) < count
        block = jnp.where(keep[:, None], block.astype(jnp.float32), jnp.float32(0.0))
        gram = lax.dot_general(block.astype(jnp.float32), block.astype(jnp.float32), (((0,), (0,)), ((), ())), precision=lax.Precision.HIGHEST, preferred_element_type=jnp.float32)
        return whiten(gram, count.astype(jnp.float32))
    return lax.map(one_expert, expert_iota)
```

```python
import jax
import jax.numpy as jnp
from jax import lax
from jax.experimental import pallas as pl
from jax.experimental.pallas import tpu as pltpu
from jax.sharding import PartitionSpec as P

damping = 0.1
BLK = 128
SUB = 8
WINDOW = 3

NN = (((1,), (0,)), ((), ()))
NT = (((1,), (1,)), ((), ()))
TN = (((0,), (0,)), ((), ()))


def split(a):
    hi = a.astype(jnp.bfloat16)
    lo = (a - hi.astype(jnp.float32)).astype(jnp.bfloat16)
    return hi, lo


def dot3(a, b, dims):
    ah, al = a
    bh, bl = b
    d = lambda x, y: lax.dot_general(x, y, dims, preferred_element_type=jnp.float32)
    return d(ah, bh) + (d(ah, bl) + d(al, bh))


def diag_inverse(block):
    count = BLK // SUB
    sub = lax.broadcasted_iota(jnp.int32, (SUB, BLK), 0)
    lane = lax.broadcasted_iota(jnp.int32, (SUB, BLK), 1)
    spread = lambda x: jnp.broadcast_to(x, (SUB, BLK))
    rows = [block[SUB * r : SUB * (r + 1), :] for r in range(count)]
    for p in range(count):
        c0 = SUB * p
        inside = (lane >= c0) & (lane < c0 + SUB)
        cols = [[spread(rows[r][:, c0 + s : c0 + s + 1]) for s in range(SUB)] for r in range(p, count)]
        rows[p] = jnp.where(inside, jnp.where(lane - c0 == sub, 1.0, 0.0), rows[p])
        for r in range(p + 1, count):
            rows[r] = jnp.where(inside, 0.0, rows[r])
        pivots = jnp.ones((SUB, BLK), jnp.float32)
        tops, mults, heads = [], [], []
        for s in range(SUB):
            top = [spread(cols[0][t][s : s + 1, :]) for t in range(s, SUB)]
            inv = 1.0 / top[0]
            pivots = jnp.where(sub == s, top[0], pivots)
            head = spread(rows[p][s : s + 1, :])
            m = jnp.where(sub > s, cols[0][s] * inv, 0.0)
            for t in range(s + 1, SUB):
                cols[0][t] = cols[0][t] - m * top[t - s]
            rows[p] = rows[p] - m * head
            tops.append(top)
            mults.append(inv)
            heads.append(head)
        for r in range(p + 1, count):
            col = cols[r - p]
            acc = rows[r]
            for s in range(SUB):
                m = col[s] * mults[s]
                for t in range(s + 1, SUB):
                    col[t] = col[t] - m * tops[s][t - s]
                acc = acc - m * heads[s]
            rows[r] = acc
        rows[p] = jnp.where(lane <= c0 + sub, rows[p] * lax.rsqrt(pivots), 0.0)
    return jnp.concatenate(rows, axis=0)


def whole_block(x_ref, wh, wl, i, inv_count, shift):
    a = i * BLK
    eye = (
        lax.broadcasted_iota(jnp.int32, (BLK, BLK), 0) == lax.broadcasted_iota(jnp.int32, (BLK, BLK), 1)
    ).astype(jnp.float32)
    gram = lax.dot_general(x_ref[:, a : a + BLK], x_ref[:, : a + BLK], TN, preferred_element_type=jnp.float32)
    s = gram[:, a:] * inv_count + shift * eye
    if not i:
        return s, None
    g_hi, g_lo = split(gram[:, :a] * inv_count[:, 0:1])
    cuts = [(j, min(j + 2 * BLK, a)) for j in range(0, a, 2 * BLK)]
    low = jnp.concatenate(
        [dot3((g_hi[:, :e], g_lo[:, :e]), (wh[j:e, :e], wl[j:e, :e]), NT) for j, e in cuts], axis=1
    )
    l_hi, l_lo = split(low)
    s = s - dot3((l_hi, l_lo), (l_hi, l_lo), NT)
    t = jnp.concatenate(
        [dot3((l_hi[:, j:], l_lo[:, j:]), (wh[j:a, j:e], wl[j:a, j:e]), NN) for j, e in cuts], axis=1
    )
    return s, t


def exchange_kernel(
    ids_ref, in_hbm, o_ref, wh, wl, x_ref, scale_ref, in_ref, s_ref, t_ref, pick, outbox, inbox, stat_out, stat_in,
    in_sem, send_sem, recv_sem, stat_sem,
):
    n = x_ref.shape[1]
    steps = n // BLK
    _, devices, slots, _ = outbox.shape
    top_count, token_rows = ids_ref.shape
    entries = token_rows * top_count
    exp_size = lax.axis_size("exp")
    me = lax.axis_index("tok") * exp_size + lax.axis_index("exp")

    def place(offset):
        peer = lax.rem(me + offset, devices)
        return peer, (peer // exp_size, lax.rem(peer, exp_size))

    def part_of(c):
        part = in_ref[:, :, c * BLK : (c + 1) * BLK].astype(jnp.float32)
        return part.reshape(entries, BLK)

    barrier = pltpu.get_barrier_semaphore()

    def greet(offset, carry):
        pl.semaphore_signal(barrier, inc=1, device_id=place(offset)[1], device_id_type=pl.DeviceIdType.MESH)
        return carry

    load = pltpu.make_async_copy(in_hbm, in_ref, in_sem)
    load.start()
    lax.fori_loop(1, devices, greet, 0)

    lane = lax.broadcasted_iota(jnp.int32, (token_rows, entries), 1)
    token = lax.broadcasted_iota(jnp.int32, (token_rows, entries), 0)
    widen = (lane // top_count == token).astype(jnp.float32).astype(jnp.bfloat16)
    wide = lax.dot_general(
        ids_ref[...].astype(jnp.float32).astype(jnp.bfloat16), widen, NN, preferred_element_type=jnp.float32
    )
    choice = lax.broadcasted_iota(jnp.int32, (top_count, entries), 1) % top_count
    own_choice = choice == lax.broadcasted_iota(jnp.int32, (top_count, entries), 0)
    ids = jnp.sum(jnp.where(own_choice, wide, 0.0), axis=0, keepdims=True).astype(jnp.int32)
    onehot = lax.broadcasted_iota(jnp.int32, (devices, entries), 0) == ids
    onehot_f = onehot.astype(jnp.float32)
    onehot_b = onehot_f.astype(jnp.bfloat16)
    earlier = (
        lax.broadcasted_iota(jnp.int32, (entries, entries), 0)
        < lax.broadcasted_iota(jnp.int32, (entries, entries), 1)
    ).astype(jnp.float32).astype(jnp.bfloat16)
    before = lax.dot_general(onehot_b, earlier, NN, preferred_element_type=jnp.float32)
    rank = jnp.sum(before * onehot_f, axis=0, keepdims=True).astype(jnp.int32)
    target = ids * slots + rank
    for i in range(0, devices * slots, BLK):
        row = lax.broadcasted_iota(jnp.int32, (BLK, entries), 0) + i
        pick[i : i + BLK, :] = (row == target).astype(jnp.float32).astype(jnp.bfloat16)
    load.wait()

    def build(c):
        part = lax.dot_general(
            pick[...], part_of(c).astype(jnp.bfloat16), NN, preferred_element_type=jnp.float32
        )
        outbox[c] = part.reshape(devices, slots, BLK).astype(jnp.bfloat16)
        inbox[c, me] = outbox[c, me]

    def send(c):
        def one(offset, carry):
            peer, device = place(offset)
            pltpu.make_async_remote_copy(
                src_ref=outbox.at[c, peer],
                dst_ref=inbox.at[c, me],
                send_sem=send_sem.at[c],
                recv_sem=recv_sem.at[c],
                device_id=device,
                device_id_type=pl.DeviceIdType.MESH,
            ).start()
            return carry

        lax.fori_loop(1, devices, one, 0)

    def send_stats(offset, carry):
        peer, device = place(offset)
        pltpu.make_async_remote_copy(
            src_ref=stat_out.at[peer],
            dst_ref=stat_in.at[me],
            send_sem=stat_sem.at[0],
            recv_sem=stat_sem.at[1],
            device_id=device,
            device_id_type=pl.DeviceIdType.MESH,
        ).start()
        return carry

    build(0)
    build(1)
    pl.semaphore_wait(barrier, devices - 1)
    send(0)
    counts = jnp.sum(onehot_f, axis=1, keepdims=True)
    squares = jnp.zeros((devices, BLK), jnp.float32)
    for c in range(steps):
        v = part_of(c)
        hi, lo = split(v * v)
        squares = squares + lax.dot_general(onehot_b, hi, NN, preferred_element_type=jnp.float32)
        squares = squares + lax.dot_general(onehot_b, lo, NN, preferred_element_type=jnp.float32)
    squares = jnp.sum(squares, axis=1, keepdims=True)
    first = lax.broadcasted_iota(jnp.int32, (devices, BLK), 1) < BLK // 2
    stats = jnp.where(first, jnp.broadcast_to(counts, (devices, BLK)), jnp.broadcast_to(squares, (devices, BLK)))
    for d in range(devices):
        stat_out[d] = stats[d : d + 1, :]
    stat_in[me] = stat_out[me]

    for c in range(2, min(3, steps)):
        build(c)
    lax.fori_loop(1, devices, send_stats, 0)
    for c in range(1, min(WINDOW, steps)):
        send(c)
    for c in range(3, steps):
        build(c)
    o_ref[...] = jnp.zeros_like(o_ref)
    wh[...] = jnp.zeros_like(wh)
    wl[...] = jnp.zeros_like(wl)

    def settle(ref, sem):
        part = ref.at[pl.ds(0, devices - 1)]
        pltpu.make_async_copy(part, part, sem).wait()

    settle(stat_in, stat_sem.at[1])
    total = stat_in[0]
    for d in range(1, devices):
        total = total + stat_in[d]
    spread = lambda x: jnp.broadcast_to(x, (SUB, BLK))
    inv_count = 1.0 / spread(total[:, 0:1])
    shift = damping * (spread(total[:, BLK // 2 : BLK // 2 + 1]) * inv_count / n)
    scale_ref[0] = inv_count
    scale_ref[1] = shift
    inv_count, shift = inv_count[0:1, :], shift[0:1, :]

    def take(k):
        settle(inbox.at[k], recv_sem.at[k])
        x_ref[:, pl.ds(pl.multiple_of(k * BLK, BLK), BLK)] = (
            inbox[k].astype(jnp.float32).reshape(devices * slots, BLK).astype(jnp.bfloat16)
        )

    def step(k, carry):
        base = pl.multiple_of(k * BLK, BLK)

        @pl.when(k + WINDOW < steps)
        def _():
            send(k + WINDOW)

        take(k)
        for i in range(steps - 1):

            @pl.when(k == i)
            def _():
                s, t = whole_block(x_ref, wh, wl, i, inv_count, shift)
                s_ref[...] = s
                if i:
                    t_ref[:, : i * BLK] = t

        own = diag_inverse(s_ref[...])
        at = (pl.ds(base, BLK), pl.ds(base, BLK))
        o_ref[at] = own
        own_hi, own_lo = split(own)
        wh[at] = own_hi
        wl[at] = own_lo
        for i in range(1, steps - 1):

            @pl.when(k == i)
            def _():
                a = i * BLK
                row = -dot3((own_hi, own_lo), split(t_ref[:, :a]), NN)
                o_ref[a : a + BLK, :a] = row
                hi, lo = split(row)
                wh[a : a + BLK, :a] = hi
                wl[a : a + BLK, :a] = lo

        return carry

    lax.fori_loop(0, steps - 1, step, 0)
    settle(stat_out, stat_sem.at[0])

    def drain(c, carry):
        settle(outbox.at[c], send_sem.at[c])
        return carry

    lax.fori_loop(0, steps, drain, 0)
    take(steps - 1)


def last_kernel(o_ref, wh, wl, x_ref, scale_ref, out_ref, last, sems):
    n = x_ref.shape[1]
    done = n - BLK
    early = pltpu.make_async_copy(o_ref, out_ref.at[pl.ds(0, done)], sems.at[0])
    early.start()
    s, t = whole_block(x_ref, wh, wl, n // BLK - 1, scale_ref[0, 0:1, :], scale_ref[1, 0:1, :])
    own = diag_inverse(s)
    last[:, done:] = own
    last[:, :done] = -dot3(split(own), split(t), NN)
    late = pltpu.make_async_copy(last, out_ref.at[pl.ds(done, BLK)], sems.at[1])
    late.start()
    early.wait()
    late.wait()


def shards(captured, expert_ids):
    devices = lax.axis_size("tok") * lax.axis_size("exp")
    token_rows, top_count, n = captured.shape
    entries = token_rows * top_count
    slots = 2 * entries // devices
    steps = n // BLK
    done = n - BLK
    vmem = pl.BlockSpec(memory_space=pltpu.VMEM)
    hbm = pl.BlockSpec(memory_space=pltpu.HBM)
    bf16, f32 = jnp.bfloat16, jnp.float32
    box = pltpu.VMEM((steps, devices, slots, BLK), bf16)
    stat = pltpu.VMEM((devices, 1, BLK), f32)
    parts = pl.pallas_call(
        exchange_kernel,
        out_shape=[
            pltpu.VMEM((done, n), f32),
            pltpu.VMEM((done, done), bf16),
            pltpu.VMEM((done, done), bf16),
            pltpu.VMEM((devices * slots, n), bf16),
            pltpu.VMEM((2, SUB, BLK), f32),
        ],
        in_specs=[vmem, hbm],
        out_specs=[vmem] * 5,
        scratch_shapes=[
            pltpu.VMEM((token_rows, top_count, n), bf16),
            pltpu.VMEM((BLK, BLK), f32),
            pltpu.VMEM((BLK, n), f32),
            pltpu.VMEM((devices * slots, entries), bf16),
            box,
            box,
            stat,
            stat,
            pltpu.SemaphoreType.DMA,
            pltpu.SemaphoreType.DMA((steps,)),
            pltpu.SemaphoreType.DMA((steps,)),
            pltpu.SemaphoreType.DMA((2,)),
        ],
        compiler_params=pltpu.CompilerParams(collective_id=0, has_side_effects=True, vmem_limit_bytes=50 << 20),
        name="exchange_whiten",
    )(expert_ids.T, captured)
    out = pl.pallas_call(
        last_kernel,
        out_shape=jax.ShapeDtypeStruct((n, n), f32),
        in_specs=[vmem] * 5,
        out_specs=pl.BlockSpec(memory_space=pl.ANY),
        scratch_shapes=[pltpu.VMEM((BLK, n), f32), pltpu.SemaphoreType.DMA((2,))],
        compiler_params=pltpu.CompilerParams(vmem_limit_bytes=36 << 20),
        name="whiten_last",
    )(*parts)
    return out[None]


def solution(mesh):
    placed = (P(("tok", "exp"), None, None), P(("tok", "exp"), None))
    return jax.shard_map(
        shards, mesh=mesh, in_specs=placed, out_specs=P(("tok", "exp"), None, None), check_vma=False
    )
```

```python
import jax
import jax.numpy as jnp
from jax import lax
from jax.experimental import pallas as pl
from jax.experimental.pallas import tpu as pltpu
from jax.sharding import PartitionSpec as P

damping = 0.1
BLK = 128
SUB = 8
PAN = 32
WINDOW = 3

NN = (((1,), (0,)), ((), ()))
NT = (((1,), (1,)), ((), ()))
TN = (((0,), (0,)), ((), ()))


def split(a):
    hi = a.astype(jnp.bfloat16)
    lo = (a - hi.astype(jnp.float32)).astype(jnp.bfloat16)
    return hi, lo


def dot3(a, b, dims):
    ah, al = a
    bh, bl = b
    d = lambda x, y: lax.dot_general(x, y, dims, preferred_element_type=jnp.float32)
    return d(ah, bh) + (d(ah, bl) + d(al, bh))


def diag_inverse(full):
    n = full.shape[0]
    size = min(PAN, n)
    count = size // SUB
    sub = lax.broadcasted_iota(jnp.int32, (SUB, n), 0)
    lane = lax.broadcasted_iota(jnp.int32, (SUB, n), 1)
    zero = (sub * 0).astype(jnp.float32)
    spread = lambda x: jnp.broadcast_to(x, (SUB, n))
    columns = lambda v, c: [spread(v[:, c + t : c + t + 1]) + zero for t in range(SUB)]
    out = []
    for b0 in range(0, n, size):
        rows = [full[SUB * r : SUB * (r + 1), :] for r in range(count)]
        own = columns(rows[0], b0)
        side = columns(rows[1], b0)
        after = columns(rows[1], b0 + SUB)
        for p in range(count):
            c0 = b0 + SUB * p
            more = p + 1 < count
            inside = (lane >= c0) & (lane < c0 + SUB)
            row = jnp.where(inside, jnp.where(lane - c0 == sub, 1.0, 0.0), rows[p])
            below = jnp.where(inside, 0.0, rows[p + 1]) if more else None
            tops, invs, heads = [], [], []
            pivots = None
            for s in range(SUB):
                top = {t: spread(own[s][t : t + 1, :]) for t in range(s, SUB)}
                inv = 1.0 / top[s]
                pivots = jnp.where(sub >= s, top[s], pivots) if s else top[s]
                head = spread(row[s : s + 1, :])
                if s < SUB - 1:
                    m = jnp.where(sub > s, own[s] * inv, 0.0)
                    for t in range(s + 1, SUB):
                        own[t] = own[t] - m * top[t]
                    row = row - m * head
                if more:
                    x = side[s]
                    m = x * inv
                    for t in range(s + 1, SUB):
                        side[t] = side[t] - m * top[t]
                    below = below - m * head
                    for t in range(SUB):
                        after[t] = after[t] - m * spread(x[t : t + 1, :])
                tops.append(top)
                invs.append(inv)
                heads.append(head)
            rows[p] = row * lax.rsqrt(pivots)
            if more:
                rows[p + 1] = below
            own = after
            if p + 2 < count:
                solved = [None] * SUB
                for t in range(SUB - 1, -1, -1):
                    v = heads[t]
                    for k in range(SUB - 1, t, -1):
                        v = v - tops[t][k] * solved[k]
                    solved[t] = v * invs[t]
                for r in range(p + 2, count):
                    acc = jnp.where(inside, 0.0, rows[r])
                    for col, v in zip(columns(rows[r], c0), solved):
                        acc = acc - col * v
                    rows[r] = acc
                side = columns(rows[p + 2], c0 + SUB)
                after = columns(rows[p + 2], c0 + 2 * SUB)
        lower = [jnp.where(lane <= b0 + SUB * p + sub, rows[p], 0.0) for p in range(count)]
        out += lower
        if b0 + size < n:
            both = jnp.concatenate(
                [jnp.where(lane >= b0 + size, rows[p], lower[p]) for p in range(count)], axis=0
            )
            hi, lo = split(both)
            update = lax.dot_general(
                jnp.concatenate([hi, hi, lo], axis=0),
                jnp.concatenate([hi, lo, hi], axis=0),
                TN,
                preferred_element_type=jnp.float32,
            )
            rest = full[size:, :]
            spot = lax.broadcasted_iota(jnp.int32, rest.shape, 1)
            full = jnp.where((spot >= b0) & (spot < b0 + size), 0.0, rest) - update[b0 + size :, :]
    return jnp.concatenate(out, axis=0)


def whole_block(x_ref, wh, wl, i, inv_count, shift):
    a = i * BLK
    eye = (
        lax.broadcasted_iota(jnp.int32, (BLK, BLK), 0) == lax.broadcasted_iota(jnp.int32, (BLK, BLK), 1)
    ).astype(jnp.float32)
    gram = lax.dot_general(x_ref[:, a : a + BLK], x_ref[:, : a + BLK], TN, preferred_element_type=jnp.float32)
    s = gram[:, a:] * inv_count + shift * eye
    if not i:
        return s, None
    g_hi, g_lo = split(gram[:, :a] * inv_count[:, 0:1])
    cuts = [(j, min(j + 2 * BLK, a)) for j in range(0, a, 2 * BLK)]
    low = jnp.concatenate(
        [dot3((g_hi[:, :e], g_lo[:, :e]), (wh[j:e, :e], wl[j:e, :e]), NT) for j, e in cuts], axis=1
    )
    l_hi, l_lo = split(low)
    s = s - dot3((l_hi, l_lo), (l_hi, l_lo), NT)
    t = jnp.concatenate(
        [dot3((l_hi[:, j:], l_lo[:, j:]), (wh[j:a, j:e], wl[j:a, j:e]), NN) for j, e in cuts], axis=1
    )
    return s, t


def exchange_kernel(
    ids_ref, in_hbm, o_ref, wh, wl, x_ref, scale_ref, in_ref, s_ref, t_ref, pick, outbox, inbox, stat_out, stat_in,
    in_sem, send_sem, recv_sem, stat_sem,
):
    n = x_ref.shape[1]
    steps = n // BLK
    _, devices, slots, _ = outbox.shape
    top_count, token_rows = ids_ref.shape
    entries = token_rows * top_count
    exp_size = lax.axis_size("exp")
    me = lax.axis_index("tok") * exp_size + lax.axis_index("exp")

    def place(offset):
        peer = lax.rem(me + offset, devices)
        return peer, (peer // exp_size, lax.rem(peer, exp_size))

    def part_of(c):
        part = in_ref[:, :, c * BLK : (c + 1) * BLK].astype(jnp.float32)
        return part.reshape(entries, BLK)

    barrier = pltpu.get_barrier_semaphore()

    def greet(offset, carry):
        pl.semaphore_signal(barrier, inc=1, device_id=place(offset)[1], device_id_type=pl.DeviceIdType.MESH)
        return carry

    load = pltpu.make_async_copy(in_hbm, in_ref, in_sem)
    load.start()
    lax.fori_loop(1, devices, greet, 0)

    lane = lax.broadcasted_iota(jnp.int32, (token_rows, entries), 1)
    token = lax.broadcasted_iota(jnp.int32, (token_rows, entries), 0)
    widen = (lane // top_count == token).astype(jnp.float32).astype(jnp.bfloat16)
    wide = lax.dot_general(
        ids_ref[...].astype(jnp.float32).astype(jnp.bfloat16), widen, NN, preferred_element_type=jnp.float32
    )
    choice = lax.broadcasted_iota(jnp.int32, (top_count, entries), 1) % top_count
    own_choice = choice == lax.broadcasted_iota(jnp.int32, (top_count, entries), 0)
    ids = jnp.sum(jnp.where(own_choice, wide, 0.0), axis=0, keepdims=True).astype(jnp.int32)
    onehot = lax.broadcasted_iota(jnp.int32, (devices, entries), 0) == ids
    onehot_f = onehot.astype(jnp.float32)
    onehot_b = onehot_f.astype(jnp.bfloat16)
    earlier = (
        lax.broadcasted_iota(jnp.int32, (entries, entries), 0)
        < lax.broadcasted_iota(jnp.int32, (entries, entries), 1)
    ).astype(jnp.float32).astype(jnp.bfloat16)
    before = lax.dot_general(onehot_b, earlier, NN, preferred_element_type=jnp.float32)
    rank = jnp.sum(before * onehot_f, axis=0, keepdims=True).astype(jnp.int32)
    target = ids * slots + rank
    for i in range(0, devices * slots, BLK):
        row = lax.broadcasted_iota(jnp.int32, (BLK, entries), 0) + i
        pick[i : i + BLK, :] = (row == target).astype(jnp.float32).astype(jnp.bfloat16)
    load.wait()

    def build(c):
        part = lax.dot_general(
            pick[...], part_of(c).astype(jnp.bfloat16), NN, preferred_element_type=jnp.float32
        )
        outbox[c] = part.reshape(devices, slots, BLK).astype(jnp.bfloat16)
        inbox[c, me] = outbox[c, me]

    def send(c):
        def one(offset, carry):
            peer, device = place(offset)
            pltpu.make_async_remote_copy(
                src_ref=outbox.at[c, peer],
                dst_ref=inbox.at[c, me],
                send_sem=send_sem.at[c],
                recv_sem=recv_sem.at[c],
                device_id=device,
                device_id_type=pl.DeviceIdType.MESH,
            ).start()
            return carry

        lax.fori_loop(1, devices, one, 0)

    def send_stats(offset, carry):
        peer, device = place(offset)
        pltpu.make_async_remote_copy(
            src_ref=stat_out.at[peer],
            dst_ref=stat_in.at[me],
            send_sem=stat_sem.at[0],
            recv_sem=stat_sem.at[1],
            device_id=device,
            device_id_type=pl.DeviceIdType.MESH,
        ).start()
        return carry

    build(0)
    build(1)
    pl.semaphore_wait(barrier, devices - 1)
    send(0)
    counts = jnp.sum(onehot_f, axis=1, keepdims=True)
    squares = jnp.zeros((devices, BLK), jnp.float32)
    for c in range(steps):
        v = part_of(c)
        hi, lo = split(v * v)
        squares = squares + lax.dot_general(onehot_b, hi, NN, preferred_element_type=jnp.float32)
        squares = squares + lax.dot_general(onehot_b, lo, NN, preferred_element_type=jnp.float32)
    squares = jnp.sum(squares, axis=1, keepdims=True)
    first = lax.broadcasted_iota(jnp.int32, (devices, BLK), 1) < BLK // 2
    stats = jnp.where(first, jnp.broadcast_to(counts, (devices, BLK)), jnp.broadcast_to(squares, (devices, BLK)))
    for d in range(devices):
        stat_out[d] = stats[d : d + 1, :]
    stat_in[me] = stat_out[me]

    for c in range(2, min(3, steps)):
        build(c)
    lax.fori_loop(1, devices, send_stats, 0)
    for c in range(1, min(WINDOW, steps)):
        send(c)
    for c in range(3, steps):
        build(c)
    o_ref[...] = jnp.zeros_like(o_ref)
    wh[...] = jnp.zeros_like(wh)
    wl[...] = jnp.zeros_like(wl)

    def settle(ref, sem):
        part = ref.at[pl.ds(0, devices - 1)]
        pltpu.make_async_copy(part, part, sem).wait()

    settle(stat_in, stat_sem.at[1])
    total = stat_in[0]
    for d in range(1, devices):
        total = total + stat_in[d]
    spread = lambda x: jnp.broadcast_to(x, (SUB, BLK))
    inv_count = 1.0 / spread(total[:, 0:1])
    shift = damping * (spread(total[:, BLK // 2 : BLK // 2 + 1]) * inv_count / n)
    scale_ref[0] = inv_count
    scale_ref[1] = shift
    inv_count, shift = inv_count[0:1, :], shift[0:1, :]

    def take(k):
        settle(inbox.at[k], recv_sem.at[k])
        x_ref[:, pl.ds(pl.multiple_of(k * BLK, BLK), BLK)] = (
            inbox[k].astype(jnp.float32).reshape(devices * slots, BLK).astype(jnp.bfloat16)
        )

    def step(k, carry):
        base = pl.multiple_of(k * BLK, BLK)

        @pl.when(k + WINDOW < steps)
        def _():
            send(k + WINDOW)

        take(k)
        for i in range(steps - 1):

            @pl.when(k == i)
            def _():
                s, t = whole_block(x_ref, wh, wl, i, inv_count, shift)
                s_ref[...] = s
                if i:
                    t_ref[:, : i * BLK] = t

        own = diag_inverse(s_ref[...])
        at = (pl.ds(base, BLK), pl.ds(base, BLK))
        o_ref[at] = own
        own_hi, own_lo = split(own)
        wh[at] = own_hi
        wl[at] = own_lo
        for i in range(1, steps - 1):

            @pl.when(k == i)
            def _():
                a = i * BLK
                row = -dot3((own_hi, own_lo), split(t_ref[:, :a]), NN)
                o_ref[a : a + BLK, :a] = row
                hi, lo = split(row)
                wh[a : a + BLK, :a] = hi
                wl[a : a + BLK, :a] = lo

        return carry

    lax.fori_loop(0, steps - 1, step, 0)
    settle(stat_out, stat_sem.at[0])

    def drain(c, carry):
        settle(outbox.at[c], send_sem.at[c])
        return carry

    lax.fori_loop(0, steps, drain, 0)
    take(steps - 1)


def last_kernel(o_ref, wh, wl, x_ref, scale_ref, out_ref, last, sems):
    n = x_ref.shape[1]
    done = n - BLK
    early = pltpu.make_async_copy(o_ref, out_ref.at[pl.ds(0, done)], sems.at[0])
    early.start()
    s, t = whole_block(x_ref, wh, wl, n // BLK - 1, scale_ref[0, 0:1, :], scale_ref[1, 0:1, :])
    own = diag_inverse(s)
    last[:, done:] = own
    last[:, :done] = -dot3(split(own), split(t), NN)
    late = pltpu.make_async_copy(last, out_ref.at[pl.ds(done, BLK)], sems.at[1])
    late.start()
    early.wait()
    late.wait()


def shards(captured, expert_ids):
    devices = lax.axis_size("tok") * lax.axis_size("exp")
    token_rows, top_count, n = captured.shape
    entries = token_rows * top_count
    slots = 2 * entries // devices
    steps = n // BLK
    done = n - BLK
    vmem = pl.BlockSpec(memory_space=pltpu.VMEM)
    hbm = pl.BlockSpec(memory_space=pltpu.HBM)
    bf16, f32 = jnp.bfloat16, jnp.float32
    box = pltpu.VMEM((steps, devices, slots, BLK), bf16)
    stat = pltpu.VMEM((devices, 1, BLK), f32)
    parts = pl.pallas_call(
        exchange_kernel,
        out_shape=[
            pltpu.VMEM((done, n), f32),
            pltpu.VMEM((done, done), bf16),
            pltpu.VMEM((done, done), bf16),
            pltpu.VMEM((devices * slots, n), bf16),
            pltpu.VMEM((2, SUB, BLK), f32),
        ],
        in_specs=[vmem, hbm],
        out_specs=[vmem] * 5,
        scratch_shapes=[
            pltpu.VMEM((token_rows, top_count, n), bf16),
            pltpu.VMEM((BLK, BLK), f32),
            pltpu.VMEM((BLK, n), f32),
            pltpu.VMEM((devices * slots, entries), bf16),
            box,
            box,
            stat,
            stat,
            pltpu.SemaphoreType.DMA,
            pltpu.SemaphoreType.DMA((steps,)),
            pltpu.SemaphoreType.DMA((steps,)),
            pltpu.SemaphoreType.DMA((2,)),
        ],
        compiler_params=pltpu.CompilerParams(collective_id=0, has_side_effects=True, vmem_limit_bytes=50 << 20),
        name="exchange_whiten",
    )(expert_ids.T, captured)
    out = pl.pallas_call(
        last_kernel,
        out_shape=jax.ShapeDtypeStruct((n, n), f32),
        in_specs=[vmem] * 5,
        out_specs=pl.BlockSpec(memory_space=pl.ANY),
        scratch_shapes=[pltpu.VMEM((BLK, n), f32), pltpu.SemaphoreType.DMA((2,))],
        compiler_params=pltpu.CompilerParams(vmem_limit_bytes=36 << 20),
        name="whiten_last",
    )(*parts)
    return out[None]


def solution(mesh):
    placed = (P(("tok", "exp"), None, None), P(("tok", "exp"), None))
    return jax.shard_map(
        shards, mesh=mesh, in_specs=placed, out_specs=P(("tok", "exp"), None, None), check_vma=False
    )
```

```python
import jax
import jax.numpy as jnp
from jax import lax
from jax.experimental import pallas as pl
from jax.experimental.pallas import tpu as pltpu
from jax.sharding import PartitionSpec as P

damping = 0.1
BLK = 128
SUB = 8
PAN = 32
WINDOW = 2

NN = (((1,), (0,)), ((), ()))
NT = (((1,), (1,)), ((), ()))
TN = (((0,), (0,)), ((), ()))


def split(a):
    hi = a.astype(jnp.bfloat16)
    lo = (a - hi.astype(jnp.float32)).astype(jnp.bfloat16)
    return hi, lo


def dot3(a, b, dims):
    ah, al = a
    bh, bl = b
    d = lambda x, y: lax.dot_general(x, y, dims, preferred_element_type=jnp.float32)
    return d(ah, bh) + (d(ah, bl) + d(al, bh))


def diag_inverse(full):
    n = full.shape[0]
    size = min(PAN, n)
    count = size // SUB
    sub = lax.broadcasted_iota(jnp.int32, (SUB, n), 0)
    lane = lax.broadcasted_iota(jnp.int32, (SUB, n), 1)
    zero = (sub * 0).astype(jnp.float32)
    spread = lambda x: jnp.broadcast_to(x, (SUB, n))
    columns = lambda v, c: [spread(v[:, c + t : c + t + 1]) + zero for t in range(SUB)]
    out = []
    for b0 in range(0, n, size):
        rows = [full[SUB * r : SUB * (r + 1), :] for r in range(count)]
        own = columns(rows[0], b0)
        side = columns(rows[1], b0)
        after = columns(rows[1], b0 + SUB)
        for p in range(count):
            c0 = b0 + SUB * p
            more = p + 1 < count
            inside = (lane >= c0) & (lane < c0 + SUB)
            row = jnp.where(inside, jnp.where(lane - c0 == sub, 1.0, 0.0), rows[p])
            below = jnp.where(inside, 0.0, rows[p + 1]) if more else None
            tops, invs, heads = [], [], []
            pivots = None
            for s in range(SUB):
                top = {t: spread(own[s][t : t + 1, :]) for t in range(s, SUB)}
                inv = 1.0 / top[s]
                pivots = jnp.where(sub >= s, top[s], pivots) if s else top[s]
                head = spread(row[s : s + 1, :])
                if s < SUB - 1:
                    m = jnp.where(sub > s, own[s] * inv, 0.0)
                    for t in range(s + 1, SUB):
                        own[t] = own[t] - m * top[t]
                    row = row - m * head
                if more:
                    x = side[s]
                    m = x * inv
                    for t in range(s + 1, SUB):
                        side[t] = side[t] - m * top[t]
                    below = below - m * head
                    for t in range(SUB):
                        after[t] = after[t] - m * spread(x[t : t + 1, :])
                tops.append(top)
                invs.append(inv)
                heads.append(head)
            rows[p] = row * lax.rsqrt(pivots)
            if more:
                rows[p + 1] = below
            own = after
            if p + 2 < count:
                solved = [None] * SUB
                for t in range(SUB - 1, -1, -1):
                    v = heads[t]
                    for k in range(SUB - 1, t, -1):
                        v = v - tops[t][k] * solved[k]
                    solved[t] = v * invs[t]
                for r in range(p + 2, count):
                    acc = jnp.where(inside, 0.0, rows[r])
                    for col, v in zip(columns(rows[r], c0), solved):
                        acc = acc - col * v
                    rows[r] = acc
                side = columns(rows[p + 2], c0 + SUB)
                after = columns(rows[p + 2], c0 + 2 * SUB)
        lower = [jnp.where(lane <= b0 + SUB * p + sub, rows[p], 0.0) for p in range(count)]
        out += lower
        if b0 + size < n:
            both = jnp.concatenate(
                [jnp.where(lane >= b0 + size, rows[p], lower[p]) for p in range(count)], axis=0
            )
            hi, lo = split(both)
            update = lax.dot_general(
                jnp.concatenate([hi, hi, lo], axis=0),
                jnp.concatenate([hi, lo, hi], axis=0),
                TN,
                preferred_element_type=jnp.float32,
            )
            rest = full[size:, :]
            spot = lax.broadcasted_iota(jnp.int32, rest.shape, 1)
            full = jnp.where((spot >= b0) & (spot < b0 + size), 0.0, rest) - update[b0 + size :, :]
    return jnp.concatenate(out, axis=0)


def whole_block(x_ref, wh, wl, i, inv_count, shift):
    a = i * BLK
    eye = (
        lax.broadcasted_iota(jnp.int32, (BLK, BLK), 0) == lax.broadcasted_iota(jnp.int32, (BLK, BLK), 1)
    ).astype(jnp.float32)
    gram = lax.dot_general(x_ref[:, a : a + BLK], x_ref[:, : a + BLK], TN, preferred_element_type=jnp.float32)
    s = gram[:, a:] * inv_count + shift * eye
    if not i:
        return s, None
    g_hi, g_lo = split(gram[:, :a] * inv_count[:, 0:1])
    cuts = [(j, min(j + 2 * BLK, a)) for j in range(0, a, 2 * BLK)]
    low = jnp.concatenate(
        [dot3((g_hi[:, :e], g_lo[:, :e]), (wh[j:e, :e], wl[j:e, :e]), NT) for j, e in cuts], axis=1
    )
    l_hi, l_lo = split(low)
    s = s - dot3((l_hi, l_lo), (l_hi, l_lo), NT)
    t = jnp.concatenate(
        [dot3((l_hi[:, j:], l_lo[:, j:]), (wh[j:a, j:e], wl[j:a, j:e]), NN) for j, e in cuts], axis=1
    )
    return s, t


def exchange_kernel(
    ids_ref, in_hbm, o_ref, wh, wl, x_ref, scale_ref, in_ref, s_ref, t_ref, pick, outbox, inbox, stat_out, stat_in,
    in_sem, send_sem, recv_sem, stat_sem,
):
    n = x_ref.shape[1]
    steps = n // BLK
    _, devices, slots, _ = outbox.shape
    top_count, token_rows = ids_ref.shape
    entries = token_rows * top_count
    exp_size = lax.axis_size("exp")
    me = lax.axis_index("tok") * exp_size + lax.axis_index("exp")

    def place(offset):
        peer = lax.rem(me + offset, devices)
        return peer, (peer // exp_size, lax.rem(peer, exp_size))

    def part_of(c):
        part = in_ref[:, :, c * BLK : (c + 1) * BLK].astype(jnp.float32)
        return part.reshape(entries, BLK)

    barrier = pltpu.get_barrier_semaphore()

    def greet(offset, carry):
        pl.semaphore_signal(barrier, inc=1, device_id=place(offset)[1], device_id_type=pl.DeviceIdType.MESH)
        return carry

    load = pltpu.make_async_copy(in_hbm, in_ref, in_sem)
    load.start()
    def far_first(step, carry):
        exp, tok = lax.axis_index("exp"), lax.axis_index("tok")
        toks = devices // exp_size
        j = step // toks
        peer_exp = lax.select(exp >= exp_size // 2, j, exp_size - 1 - j)
        peer_tok = lax.rem(toks - 1 - tok + lax.rem(step, toks), toks)

        @pl.when((peer_exp != exp) | (peer_tok != tok))
        def _():
            pl.semaphore_signal(barrier, inc=1, device_id=(peer_tok, peer_exp), device_id_type=pl.DeviceIdType.MESH)

        return carry

    lax.fori_loop(0, devices, far_first, 0)

    lane = lax.broadcasted_iota(jnp.int32, (token_rows, entries), 1)
    token = lax.broadcasted_iota(jnp.int32, (token_rows, entries), 0)
    widen = (lane // top_count == token).astype(jnp.float32).astype(jnp.bfloat16)
    wide = lax.dot_general(
        ids_ref[...].astype(jnp.float32).astype(jnp.bfloat16), widen, NN, preferred_element_type=jnp.float32
    )
    choice = lax.broadcasted_iota(jnp.int32, (top_count, entries), 1) % top_count
    own_choice = choice == lax.broadcasted_iota(jnp.int32, (top_count, entries), 0)
    ids = jnp.sum(jnp.where(own_choice, wide, 0.0), axis=0, keepdims=True).astype(jnp.int32)
    onehot = lax.broadcasted_iota(jnp.int32, (devices, entries), 0) == ids
    onehot_f = onehot.astype(jnp.float32)
    onehot_b = onehot_f.astype(jnp.bfloat16)
    earlier = (
        lax.broadcasted_iota(jnp.int32, (entries, entries), 0)
        < lax.broadcasted_iota(jnp.int32, (entries, entries), 1)
    ).astype(jnp.float32).astype(jnp.bfloat16)
    before = lax.dot_general(onehot_b, earlier, NN, preferred_element_type=jnp.float32)
    rank = jnp.sum(before * onehot_f, axis=0, keepdims=True).astype(jnp.int32)
    target = ids * slots + rank
    for i in range(0, devices * slots, BLK):
        row = lax.broadcasted_iota(jnp.int32, (BLK, entries), 0) + i
        pick[i : i + BLK, :] = (row == target).astype(jnp.float32).astype(jnp.bfloat16)
    load.wait()

    def build(c):
        part = lax.dot_general(
            pick[...], part_of(c).astype(jnp.bfloat16), NN, preferred_element_type=jnp.float32
        )
        outbox[c] = part.reshape(devices, slots, BLK).astype(jnp.bfloat16)
        inbox[c, me] = outbox[c, me]

    def send(c):
        def one(offset, carry):
            peer, device = place(offset)
            pltpu.make_async_remote_copy(
                src_ref=outbox.at[c, peer],
                dst_ref=inbox.at[c, me],
                send_sem=send_sem.at[c],
                recv_sem=recv_sem.at[c],
                device_id=device,
                device_id_type=pl.DeviceIdType.MESH,
            ).start()
            return carry

        lax.fori_loop(1, devices, one, 0)

    def send_stats(offset, carry):
        peer, device = place(offset)
        pltpu.make_async_remote_copy(
            src_ref=stat_out.at[peer],
            dst_ref=stat_in.at[me],
            send_sem=stat_sem.at[0],
            recv_sem=stat_sem.at[1],
            device_id=device,
            device_id_type=pl.DeviceIdType.MESH,
        ).start()
        return carry

    build(0)
    build(1)
    pl.semaphore_wait(barrier, devices - 1)
    send(0)
    counts = jnp.sum(onehot_f, axis=1, keepdims=True)
    squares = jnp.zeros((devices, BLK), jnp.float32)
    for c in range(steps):
        v = part_of(c)
        hi, lo = split(v * v)
        squares = squares + lax.dot_general(onehot_b, hi, NN, preferred_element_type=jnp.float32)
        squares = squares + lax.dot_general(onehot_b, lo, NN, preferred_element_type=jnp.float32)
    squares = jnp.sum(squares, axis=1, keepdims=True)
    first = lax.broadcasted_iota(jnp.int32, (devices, BLK), 1) < BLK // 2
    stats = jnp.where(first, jnp.broadcast_to(counts, (devices, BLK)), jnp.broadcast_to(squares, (devices, BLK)))
    for d in range(devices):
        stat_out[d] = stats[d : d + 1, :]
    stat_in[me] = stat_out[me]

    for c in range(2, min(3, steps)):
        build(c)
    lax.fori_loop(1, devices, send_stats, 0)
    for c in range(1, min(WINDOW, steps)):
        send(c)
    for c in range(3, steps):
        build(c)
    o_ref[...] = jnp.zeros_like(o_ref)
    wh[...] = jnp.zeros_like(wh)
    wl[...] = jnp.zeros_like(wl)

    def settle(ref, sem):
        part = ref.at[pl.ds(0, devices - 1)]
        pltpu.make_async_copy(part, part, sem).wait()

    settle(stat_in, stat_sem.at[1])
    total = stat_in[0]
    for d in range(1, devices):
        total = total + stat_in[d]
    spread = lambda x: jnp.broadcast_to(x, (SUB, BLK))
    inv_count = 1.0 / spread(total[:, 0:1])
    shift = damping * (spread(total[:, BLK // 2 : BLK // 2 + 1]) * inv_count / n)
    scale_ref[0] = inv_count
    scale_ref[1] = shift
    inv_count, shift = inv_count[0:1, :], shift[0:1, :]

    def take(k):
        settle(inbox.at[k], recv_sem.at[k])
        x_ref[:, pl.ds(pl.multiple_of(k * BLK, BLK), BLK)] = (
            inbox[k].astype(jnp.float32).reshape(devices * slots, BLK).astype(jnp.bfloat16)
        )

    def step(k, carry):
        base = pl.multiple_of(k * BLK, BLK)

        @pl.when(k + WINDOW < steps)
        def _():
            send(k + WINDOW)

        take(k)
        for i in range(steps - 1):

            @pl.when(k == i)
            def _():
                s, t = whole_block(x_ref, wh, wl, i, inv_count, shift)
                s_ref[...] = s
                if i:
                    t_ref[:, : i * BLK] = t

        own = diag_inverse(s_ref[...])
        at = (pl.ds(base, BLK), pl.ds(base, BLK))
        o_ref[at] = own
        own_hi, own_lo = split(own)
        wh[at] = own_hi
        wl[at] = own_lo
        for i in range(1, steps - 1):

            @pl.when(k == i)
            def _():
                a = i * BLK
                row = -dot3((own_hi, own_lo), split(t_ref[:, :a]), NN)
                o_ref[a : a + BLK, :a] = row
                hi, lo = split(row)
                wh[a : a + BLK, :a] = hi
                wl[a : a + BLK, :a] = lo

        return carry

    lax.fori_loop(0, steps - 1, step, 0)
    settle(stat_out, stat_sem.at[0])

    def drain(c, carry):
        settle(outbox.at[c], send_sem.at[c])
        return carry

    lax.fori_loop(0, steps, drain, 0)
    take(steps - 1)


def last_kernel(o_ref, wh, wl, x_ref, scale_ref, out_ref, last, sems):
    n = x_ref.shape[1]
    done = n - BLK
    early = pltpu.make_async_copy(o_ref, out_ref.at[pl.ds(0, done)], sems.at[0])
    early.start()
    s, t = whole_block(x_ref, wh, wl, n // BLK - 1, scale_ref[0, 0:1, :], scale_ref[1, 0:1, :])
    own = diag_inverse(s)
    last[:, done:] = own
    last[:, :done] = -dot3(split(own), split(t), NN)
    late = pltpu.make_async_copy(last, out_ref.at[pl.ds(done, BLK)], sems.at[1])
    late.start()
    early.wait()
    late.wait()


def shards(captured, expert_ids):
    devices = lax.axis_size("tok") * lax.axis_size("exp")
    token_rows, top_count, n = captured.shape
    entries = token_rows * top_count
    slots = 2 * entries // devices
    steps = n // BLK
    done = n - BLK
    vmem = pl.BlockSpec(memory_space=pltpu.VMEM)
    hbm = pl.BlockSpec(memory_space=pltpu.HBM)
    bf16, f32 = jnp.bfloat16, jnp.float32
    box = pltpu.VMEM((steps, devices, slots, BLK), bf16)
    stat = pltpu.VMEM((devices, 1, BLK), f32)
    parts = pl.pallas_call(
        exchange_kernel,
        out_shape=[
            pltpu.VMEM((done, n), f32),
            pltpu.VMEM((done, done), bf16),
            pltpu.VMEM((done, done), bf16),
            pltpu.VMEM((devices * slots, n), bf16),
            pltpu.VMEM((2, SUB, BLK), f32),
        ],
        in_specs=[vmem, hbm],
        out_specs=[vmem] * 5,
        scratch_shapes=[
            pltpu.VMEM((token_rows, top_count, n), bf16),
            pltpu.VMEM((BLK, BLK), f32),
            pltpu.VMEM((BLK, n), f32),
            pltpu.VMEM((devices * slots, entries), bf16),
            box,
            box,
            stat,
            stat,
            pltpu.SemaphoreType.DMA,
            pltpu.SemaphoreType.DMA((steps,)),
            pltpu.SemaphoreType.DMA((steps,)),
            pltpu.SemaphoreType.DMA((2,)),
        ],
        compiler_params=pltpu.CompilerParams(collective_id=0, has_side_effects=True, vmem_limit_bytes=50 << 20),
        name="exchange_whiten",
    )(expert_ids.T, captured)
    out = pl.pallas_call(
        last_kernel,
        out_shape=jax.ShapeDtypeStruct((n, n), f32),
        in_specs=[vmem] * 5,
        out_specs=pl.BlockSpec(memory_space=pl.ANY),
        scratch_shapes=[pltpu.VMEM((BLK, n), f32), pltpu.SemaphoreType.DMA((2,))],
        compiler_params=pltpu.CompilerParams(vmem_limit_bytes=36 << 20),
        name="whiten_last",
    )(*parts)
    return out[None]


def solution(mesh):
    placed = (P(("tok", "exp"), None, None), P(("tok", "exp"), None))
    return jax.shard_map(
        shards, mesh=mesh, in_specs=placed, out_specs=P(("tok", "exp"), None, None), check_vma=False
    )
```

```python
import jax
import jax.numpy as jnp
from jax import lax
from jax.experimental import pallas as pl
from jax.experimental.pallas import tpu as pltpu
from jax.sharding import PartitionSpec as P

damping = 0.1
BLK = 128
SUB = 8
PAN = 32
WINDOW = 2

NN = (((1,), (0,)), ((), ()))
NT = (((1,), (1,)), ((), ()))
TN = (((0,), (0,)), ((), ()))


def split(a):
    hi = a.astype(jnp.bfloat16)
    lo = (a - hi.astype(jnp.float32)).astype(jnp.bfloat16)
    return hi, lo


def dot3(a, b, dims):
    ah, al = a
    bh, bl = b
    d = lambda x, y: lax.dot_general(x, y, dims, preferred_element_type=jnp.float32)
    rows = ah.shape[0]
    both = d(jnp.concatenate([ah, al], axis=0), bh)
    return both[:rows] + (d(ah, bl) + both[rows:])


def diag_inverse(full):
    n = full.shape[0]
    size = min(PAN, n)
    count = size // SUB
    sub = lax.broadcasted_iota(jnp.int32, (SUB, n), 0)
    lane = lax.broadcasted_iota(jnp.int32, (SUB, n), 1)
    zero = (sub * 0).astype(jnp.float32)
    spread = lambda x: jnp.broadcast_to(x, (SUB, n))
    columns = lambda v, c: [spread(v[:, c + t : c + t + 1]) + zero for t in range(SUB)]
    out = []
    for b0 in range(0, n, size):
        rows = [full[SUB * r : SUB * (r + 1), :] for r in range(count)]
        own = columns(rows[0], b0)
        side = columns(rows[1], b0)
        after = columns(rows[1], b0 + SUB)
        for p in range(count):
            c0 = b0 + SUB * p
            more = p + 1 < count
            inside = (lane >= c0) & (lane < c0 + SUB)
            row = jnp.where(inside, jnp.where(lane - c0 == sub, 1.0, 0.0), rows[p])
            below = jnp.where(inside, 0.0, rows[p + 1]) if more else None
            tops, invs, heads = [], [], []
            pivots = None
            for s in range(SUB):
                top = {t: spread(own[s][t : t + 1, :]) for t in range(s, SUB)}
                inv = 1.0 / top[s]
                pivots = jnp.where(sub >= s, top[s], pivots) if s else top[s]
                head = spread(row[s : s + 1, :])
                if s < SUB - 1:
                    m = jnp.where(sub > s, own[s] * inv, 0.0)
                    for t in range(s + 1, SUB):
                        own[t] = own[t] - m * top[t]
                    row = row - m * head
                if more:
                    x = side[s]
                    m = x * inv
                    for t in range(s + 1, SUB):
                        side[t] = side[t] - m * top[t]
                    below = below - m * head
                    for t in range(SUB):
                        after[t] = after[t] - m * spread(x[t : t + 1, :])
                tops.append(top)
                invs.append(inv)
                heads.append(head)
            rows[p] = row * lax.rsqrt(pivots)
            if more:
                rows[p + 1] = below
            own = after
            if p + 2 < count:
                solved = [None] * SUB
                for t in range(SUB - 1, -1, -1):
                    v = heads[t]
                    for k in range(SUB - 1, t, -1):
                        v = v - tops[t][k] * solved[k]
                    solved[t] = v * invs[t]
                for r in range(p + 2, count):
                    acc = jnp.where(inside, 0.0, rows[r])
                    for col, v in zip(columns(rows[r], c0), solved):
                        acc = acc - col * v
                    rows[r] = acc
                side = columns(rows[p + 2], c0 + SUB)
                after = columns(rows[p + 2], c0 + 2 * SUB)
        lower = [jnp.where(lane <= b0 + SUB * p + sub, rows[p], 0.0) for p in range(count)]
        out += lower
        if b0 + size < n:
            both = jnp.concatenate(
                [jnp.where(lane >= b0 + size, rows[p], lower[p]) for p in range(count)], axis=0
            )
            hi, lo = split(both)
            update = lax.dot_general(
                jnp.concatenate([hi, hi, lo], axis=0),
                jnp.concatenate([hi, lo, hi], axis=0),
                TN,
                preferred_element_type=jnp.float32,
            )
            rest = full[size:, :]
            spot = lax.broadcasted_iota(jnp.int32, rest.shape, 1)
            full = jnp.where((spot >= b0) & (spot < b0 + size), 0.0, rest) - update[b0 + size :, :]
    return jnp.concatenate(out, axis=0)


def whole_block(x_ref, wh, wl, i, inv_count, shift):
    a = i * BLK
    eye = (
        lax.broadcasted_iota(jnp.int32, (BLK, BLK), 0) == lax.broadcasted_iota(jnp.int32, (BLK, BLK), 1)
    ).astype(jnp.float32)
    gram = lax.dot_general(x_ref[:, a : a + BLK], x_ref[:, : a + BLK], TN, preferred_element_type=jnp.float32)
    s = gram[:, a:] * inv_count + shift * eye
    if not i:
        return s, None
    g_hi, g_lo = split(gram[:, :a] * inv_count[:, 0:1])
    cuts = [(j, min(j + 2 * BLK, a)) for j in range(0, a, 2 * BLK)]
    low = jnp.concatenate(
        [dot3((g_hi[:, :e], g_lo[:, :e]), (wh[j:e, :e], wl[j:e, :e]), NT) for j, e in cuts], axis=1
    )
    l_hi, l_lo = split(low)
    s = s - dot3((l_hi, l_lo), (l_hi, l_lo), NT)
    t = jnp.concatenate(
        [dot3((l_hi[:, j:], l_lo[:, j:]), (wh[j:a, j:e], wl[j:a, j:e]), NN) for j, e in cuts], axis=1
    )
    return s, t


def exchange_kernel(
    ids_ref, in_hbm, o_ref, wh, wl, x_ref, scale_ref, in_ref, s_ref, t_ref, pick, outbox, inbox, stat_out, stat_in,
    in_sem, send_sem, recv_sem, stat_sem,
):
    n = x_ref.shape[1]
    steps = n // BLK
    _, devices, slots, _ = outbox.shape
    top_count, token_rows = ids_ref.shape
    entries = token_rows * top_count
    exp_size = lax.axis_size("exp")
    me = lax.axis_index("tok") * exp_size + lax.axis_index("exp")

    def place(offset):
        peer = lax.rem(me + offset, devices)
        return peer, (peer // exp_size, lax.rem(peer, exp_size))

    def part_of(c):
        part = in_ref[:, :, c * BLK : (c + 1) * BLK].astype(jnp.float32)
        return part.reshape(entries, BLK)

    barrier = pltpu.get_barrier_semaphore()

    def greet(offset, carry):
        pl.semaphore_signal(barrier, inc=1, device_id=place(offset)[1], device_id_type=pl.DeviceIdType.MESH)
        return carry

    load = pltpu.make_async_copy(in_hbm, in_ref, in_sem)
    load.start()
    def far_first(step, carry):
        exp, tok = lax.axis_index("exp"), lax.axis_index("tok")
        toks = devices // exp_size
        j = step // toks
        peer_exp = lax.select(exp >= exp_size // 2, j, exp_size - 1 - j)
        peer_tok = lax.rem(toks - 1 - tok + lax.rem(step, toks), toks)

        @pl.when((peer_exp != exp) | (peer_tok != tok))
        def _():
            pl.semaphore_signal(barrier, inc=1, device_id=(peer_tok, peer_exp), device_id_type=pl.DeviceIdType.MESH)

        return carry

    lax.fori_loop(0, devices, far_first, 0)

    lane = lax.broadcasted_iota(jnp.int32, (token_rows, entries), 1)
    token = lax.broadcasted_iota(jnp.int32, (token_rows, entries), 0)
    widen = (lane // top_count == token).astype(jnp.float32).astype(jnp.bfloat16)
    wide = lax.dot_general(
        ids_ref[...].astype(jnp.float32).astype(jnp.bfloat16), widen, NN, preferred_element_type=jnp.float32
    )
    choice = lax.broadcasted_iota(jnp.int32, (top_count, entries), 1) % top_count
    own_choice = choice == lax.broadcasted_iota(jnp.int32, (top_count, entries), 0)
    ids = jnp.sum(jnp.where(own_choice, wide, 0.0), axis=0, keepdims=True).astype(jnp.int32)
    onehot = lax.broadcasted_iota(jnp.int32, (devices, entries), 0) == ids
    onehot_f = onehot.astype(jnp.float32)
    onehot_b = onehot_f.astype(jnp.bfloat16)
    earlier = (
        lax.broadcasted_iota(jnp.int32, (entries, entries), 0)
        < lax.broadcasted_iota(jnp.int32, (entries, entries), 1)
    ).astype(jnp.float32).astype(jnp.bfloat16)
    before = lax.dot_general(onehot_b, earlier, NN, preferred_element_type=jnp.float32)
    rank = jnp.sum(before * onehot_f, axis=0, keepdims=True).astype(jnp.int32)
    target = ids * slots + rank
    for i in range(0, devices * slots, BLK):
        row = lax.broadcasted_iota(jnp.int32, (BLK, entries), 0) + i
        pick[i : i + BLK, :] = (row == target).astype(jnp.float32).astype(jnp.bfloat16)
    load.wait()

    def build(c):
        part = lax.dot_general(
            pick[...], part_of(c).astype(jnp.bfloat16), NN, preferred_element_type=jnp.float32
        )
        outbox[c] = part.reshape(devices, slots, BLK).astype(jnp.bfloat16)
        inbox[c, me] = outbox[c, me]

    def send(c):
        def one(offset, carry):
            peer, device = place(offset)
            pltpu.make_async_remote_copy(
                src_ref=outbox.at[c, peer],
                dst_ref=inbox.at[c, me],
                send_sem=send_sem.at[c],
                recv_sem=recv_sem.at[c],
                device_id=device,
                device_id_type=pl.DeviceIdType.MESH,
            ).start()
            return carry

        lax.fori_loop(1, devices, one, 0)

    def send_stats(offset, carry):
        peer, device = place(offset)
        pltpu.make_async_remote_copy(
            src_ref=stat_out.at[peer],
            dst_ref=stat_in.at[me],
            send_sem=stat_sem.at[0],
            recv_sem=stat_sem.at[1],
            device_id=device,
            device_id_type=pl.DeviceIdType.MESH,
        ).start()
        return carry

    build(0)
    build(1)
    pl.semaphore_wait(barrier, devices - 1)
    send(0)
    counts = jnp.sum(onehot_f, axis=1, keepdims=True)
    squares = jnp.zeros((devices, BLK), jnp.float32)
    for c in range(steps):
        v = part_of(c)
        hi, lo = split(v * v)
        squares = squares + lax.dot_general(onehot_b, hi, NN, preferred_element_type=jnp.float32)
        squares = squares + lax.dot_general(onehot_b, lo, NN, preferred_element_type=jnp.float32)
    squares = jnp.sum(squares, axis=1, keepdims=True)
    first = lax.broadcasted_iota(jnp.int32, (devices, BLK), 1) < BLK // 2
    stats = jnp.where(first, jnp.broadcast_to(counts, (devices, BLK)), jnp.broadcast_to(squares, (devices, BLK)))
    for d in range(devices):
        stat_out[d] = stats[d : d + 1, :]
    stat_in[me] = stat_out[me]

    for c in range(2, min(3, steps)):
        build(c)
    lax.fori_loop(1, devices, send_stats, 0)
    for c in range(1, min(WINDOW, steps)):
        send(c)
    for c in range(3, steps):
        build(c)
    o_ref[...] = jnp.zeros_like(o_ref)
    wh[...] = jnp.zeros_like(wh)
    wl[...] = jnp.zeros_like(wl)

    def settle(ref, sem):
        part = ref.at[pl.ds(0, devices - 1)]
        pltpu.make_async_copy(part, part, sem).wait()

    settle(stat_in, stat_sem.at[1])
    total = stat_in[0]
    for d in range(1, devices):
        total = total + stat_in[d]
    spread = lambda x: jnp.broadcast_to(x, (SUB, BLK))
    inv_count = 1.0 / spread(total[:, 0:1])
    shift = damping * (spread(total[:, BLK // 2 : BLK // 2 + 1]) * inv_count / n)
    scale_ref[0] = inv_count
    scale_ref[1] = shift
    inv_count, shift = inv_count[0:1, :], shift[0:1, :]

    def take(k):
        settle(inbox.at[k], recv_sem.at[k])
        x_ref[:, pl.ds(pl.multiple_of(k * BLK, BLK), BLK)] = (
            inbox[k].reshape(devices * slots, BLK)
        )

    def step(k, carry):
        base = pl.multiple_of(k * BLK, BLK)

        @pl.when(k + WINDOW < steps)
        def _():
            send(k + WINDOW)

        take(k)
        for i in range(steps - 1):

            @pl.when(k == i)
            def _():
                s, t = whole_block(x_ref, wh, wl, i, inv_count, shift)
                s_ref[...] = s
                if i:
                    t_ref[:, : i * BLK] = t

        own = diag_inverse(s_ref[...])
        at = (pl.ds(base, BLK), pl.ds(base, BLK))
        o_ref[at] = own
        own_hi, own_lo = split(own)
        wh[at] = own_hi
        wl[at] = own_lo
        for i in range(1, steps - 1):

            @pl.when(k == i)
            def _():
                a = i * BLK
                row = -dot3((own_hi, own_lo), split(t_ref[:, :a]), NN)
                o_ref[a : a + BLK, :a] = row
                hi, lo = split(row)
                wh[a : a + BLK, :a] = hi
                wl[a : a + BLK, :a] = lo

        return carry

    lax.fori_loop(0, steps - 1, step, 0)
    settle(stat_out, stat_sem.at[0])

    def drain(c, carry):
        settle(outbox.at[c], send_sem.at[c])
        return carry

    lax.fori_loop(0, steps, drain, 0)
    take(steps - 1)


def last_kernel(o_ref, wh, wl, x_ref, scale_ref, out_ref, last, sems):
    n = x_ref.shape[1]
    done = n - BLK
    early = pltpu.make_async_copy(o_ref, out_ref.at[pl.ds(0, done)], sems.at[0])
    early.start()
    s, t = whole_block(x_ref, wh, wl, n // BLK - 1, scale_ref[0, 0:1, :], scale_ref[1, 0:1, :])
    own = diag_inverse(s)
    last[:, done:] = own
    t = split(t)
    moves = [early]
    for q, b0 in enumerate(range(0, BLK, PAN)):
        e = b0 + PAN
        part = split(own[b0:e, :e])
        last[b0:e, :done] = -dot3(part, (t[0][:e], t[1][:e]), NN)
        move = pltpu.make_async_copy(last.at[pl.ds(b0, PAN)], out_ref.at[pl.ds(done + b0, PAN)], sems.at[1 + q])
        move.start()
        moves.append(move)
    for move in moves:
        move.wait()


def shards(captured, expert_ids):
    devices = lax.axis_size("tok") * lax.axis_size("exp")
    token_rows, top_count, n = captured.shape
    entries = token_rows * top_count
    slots = 2 * entries // devices
    steps = n // BLK
    done = n - BLK
    vmem = pl.BlockSpec(memory_space=pltpu.VMEM)
    hbm = pl.BlockSpec(memory_space=pltpu.HBM)
    bf16, f32 = jnp.bfloat16, jnp.float32
    box = pltpu.VMEM((steps, devices, slots, BLK), bf16)
    stat = pltpu.VMEM((devices, 1, BLK), f32)
    parts = pl.pallas_call(
        exchange_kernel,
        out_shape=[
            pltpu.VMEM((done, n), f32),
            pltpu.VMEM((done, done), bf16),
            pltpu.VMEM((done, done), bf16),
            pltpu.VMEM((devices * slots, n), bf16),
            pltpu.VMEM((2, SUB, BLK), f32),
        ],
        in_specs=[vmem, hbm],
        out_specs=[vmem] * 5,
        scratch_shapes=[
            pltpu.VMEM((token_rows, top_count, n), bf16),
            pltpu.VMEM((BLK, BLK), f32),
            pltpu.VMEM((BLK, n), f32),
            pltpu.VMEM((devices * slots, entries), bf16),
            box,
            box,
            stat,
            stat,
            pltpu.SemaphoreType.DMA,
            pltpu.SemaphoreType.DMA((steps,)),
            pltpu.SemaphoreType.DMA((steps,)),
            pltpu.SemaphoreType.DMA((2,)),
        ],
        compiler_params=pltpu.CompilerParams(collective_id=0, has_side_effects=True, vmem_limit_bytes=50 << 20),
        name="exchange_whiten",
    )(expert_ids.T, captured)
    out = pl.pallas_call(
        last_kernel,
        out_shape=jax.ShapeDtypeStruct((n, n), f32),
        in_specs=[vmem] * 5,
        out_specs=pl.BlockSpec(memory_space=pl.ANY),
        scratch_shapes=[pltpu.VMEM((BLK, n), f32), pltpu.SemaphoreType.DMA((1 + BLK // PAN,))],
        compiler_params=pltpu.CompilerParams(vmem_limit_bytes=36 << 20),
        name="whiten_last",
    )(*parts)
    return out[None]


def solution(mesh):
    placed = (P(("tok", "exp"), None, None), P(("tok", "exp"), None))
    return jax.shard_map(
        shards, mesh=mesh, in_specs=placed, out_specs=P(("tok", "exp"), None, None), check_vma=False
    )
```

```python
import jax
import jax.numpy as jnp
from jax import lax
from jax.experimental import pallas as pl
from jax.experimental.pallas import tpu as pltpu
from jax.sharding import PartitionSpec as P

damping = 0.1
BLK = 128
SUB = 8
PAN = 32
WINDOW = 2

NN = (((1,), (0,)), ((), ()))
NT = (((1,), (1,)), ((), ()))
TN = (((0,), (0,)), ((), ()))


def split(a):
    hi = a.astype(jnp.bfloat16)
    lo = (a - hi.astype(jnp.float32)).astype(jnp.bfloat16)
    return hi, lo


def dot3(a, b, dims):
    ah, al = a
    bh, bl = b
    d = lambda x, y: lax.dot_general(x, y, dims, preferred_element_type=jnp.float32)
    rows = ah.shape[0]
    both = d(jnp.concatenate([ah, al], axis=0), bh)
    return both[:rows] + (d(ah, bl) + both[rows:])


def diag_inverse(full):
    n = full.shape[0]
    size = min(PAN, n)
    count = size // SUB
    sub = lax.broadcasted_iota(jnp.int32, (SUB, n), 0)
    lane = lax.broadcasted_iota(jnp.int32, (SUB, n), 1)
    zero = (sub * 0).astype(jnp.float32)
    spread = lambda x: jnp.broadcast_to(x, (SUB, n))
    columns = lambda v, c: [spread(v[:, c + t : c + t + 1]) + zero for t in range(SUB)]
    out = []
    for b0 in range(0, n, size):
        rows = [full[SUB * r : SUB * (r + 1), :] for r in range(count)]
        own = columns(rows[0], b0)
        side = columns(rows[1], b0)
        after = columns(rows[1], b0 + SUB)
        for p in range(count):
            c0 = b0 + SUB * p
            more = p + 1 < count
            inside = (lane >= c0) & (lane < c0 + SUB)
            row = jnp.where(inside, jnp.where(lane - c0 == sub, 1.0, 0.0), rows[p])
            below = jnp.where(inside, 0.0, rows[p + 1]) if more else None
            tops, invs, heads = [], [], []
            pivots = None
            for s in range(SUB):
                top = {t: spread(own[s][t : t + 1, :]) for t in range(s, SUB)}
                inv = 1.0 / top[s]
                pivots = jnp.where(sub >= s, top[s], pivots) if s else top[s]
                head = spread(row[s : s + 1, :])
                if s < SUB - 1:
                    m = jnp.where(sub > s, own[s] * inv, 0.0)
                    for t in range(s + 1, SUB):
                        own[t] = own[t] - m * top[t]
                    row = row - m * head
                if more:
                    x = side[s]
                    m = x * inv
                    for t in range(s + 1, SUB):
                        side[t] = side[t] - m * top[t]
                    below = below - m * head
                    for t in range(SUB):
                        after[t] = after[t] - m * spread(x[t : t + 1, :])
                tops.append(top)
                invs.append(inv)
                heads.append(head)
            rows[p] = row * lax.rsqrt(pivots)
            if more:
                rows[p + 1] = below
            own = after
            if p + 2 < count:
                solved = [None] * SUB
                for t in range(SUB - 1, -1, -1):
                    v = heads[t]
                    for k in range(SUB - 1, t, -1):
                        v = v - tops[t][k] * solved[k]
                    solved[t] = v * invs[t]
                for r in range(p + 2, count):
                    acc = jnp.where(inside, 0.0, rows[r])
                    for col, v in zip(columns(rows[r], c0), solved):
                        acc = acc - col * v
                    rows[r] = acc
                side = columns(rows[p + 2], c0 + SUB)
                after = columns(rows[p + 2], c0 + 2 * SUB)
        lower = [jnp.where(lane <= b0 + SUB * p + sub, rows[p], 0.0) for p in range(count)]
        out += lower
        if b0 + size < n:
            both = jnp.concatenate(
                [jnp.where(lane >= b0 + size, rows[p], lower[p]) for p in range(count)], axis=0
            )
            hi, lo = split(both)
            update = lax.dot_general(
                jnp.concatenate([hi, hi, lo], axis=0),
                jnp.concatenate([hi, lo, hi], axis=0),
                TN,
                preferred_element_type=jnp.float32,
            )
            rest = full[size:, :]
            spot = lax.broadcasted_iota(jnp.int32, rest.shape, 1)
            full = jnp.where((spot >= b0) & (spot < b0 + size), 0.0, rest) - update[b0 + size :, :]
    return jnp.concatenate(out, axis=0)


def whole_block(x_ref, wh, wl, i, inv_count, shift):
    a = i * BLK
    eye = (
        lax.broadcasted_iota(jnp.int32, (BLK, BLK), 0) == lax.broadcasted_iota(jnp.int32, (BLK, BLK), 1)
    ).astype(jnp.float32)
    gram = lax.dot_general(x_ref[:, a : a + BLK], x_ref[:, : a + BLK], TN, preferred_element_type=jnp.float32)
    s = gram[:, a:] * inv_count + shift * eye
    if not i:
        return s, None
    g_hi, g_lo = split(gram[:, :a] * inv_count[:, 0:1])
    cuts = [(j, min(j + 2 * BLK, a)) for j in range(0, a, 2 * BLK)]
    low = jnp.concatenate(
        [dot3((g_hi[:, :e], g_lo[:, :e]), (wh[j:e, :e], wl[j:e, :e]), NT) for j, e in cuts], axis=1
    )
    l_hi, l_lo = split(low)
    s = s - dot3((l_hi, l_lo), (l_hi, l_lo), NT)
    t = jnp.concatenate(
        [dot3((l_hi[:, j:], l_lo[:, j:]), (wh[j:a, j:e], wl[j:a, j:e]), NN) for j, e in cuts], axis=1
    )
    return s, t


def exchange_kernel(
    ids_ref, in_hbm, o_ref, wh, wl, x_ref, scale_ref, in_ref, s_ref, t_ref, pick, outbox, inbox, stat_out, stat_in,
    in_sem, send_sem, recv_sem, stat_sem,
):
    n = x_ref.shape[1]
    steps = n // BLK
    _, devices, slots, _ = outbox.shape
    top_count, token_rows = ids_ref.shape
    entries = token_rows * top_count
    exp_size = lax.axis_size("exp")
    me = lax.axis_index("tok") * exp_size + lax.axis_index("exp")

    def place(offset):
        peer = lax.rem(me + offset, devices)
        return peer, (peer // exp_size, lax.rem(peer, exp_size))

    def part_of(c):
        part = in_ref[:, :, c * BLK : (c + 1) * BLK].astype(jnp.float32)
        return part.reshape(entries, BLK)

    barrier = pltpu.get_barrier_semaphore()

    def greet(offset, carry):
        pl.semaphore_signal(barrier, inc=1, device_id=place(offset)[1], device_id_type=pl.DeviceIdType.MESH)
        return carry

    load = pltpu.make_async_copy(in_hbm, in_ref, in_sem)
    load.start()
    def far_first(step, carry):
        exp, tok = lax.axis_index("exp"), lax.axis_index("tok")
        toks = devices // exp_size
        j = step // toks
        peer_exp = lax.select(exp >= exp_size // 2, j, exp_size - 1 - j)
        peer_tok = lax.rem(toks - 1 - tok + lax.rem(step, toks), toks)

        @pl.when((peer_exp != exp) | (peer_tok != tok))
        def _():
            pl.semaphore_signal(barrier, inc=1, device_id=(peer_tok, peer_exp), device_id_type=pl.DeviceIdType.MESH)

        return carry

    lax.fori_loop(0, devices, far_first, 0)

    lane = lax.broadcasted_iota(jnp.int32, (token_rows, entries), 1)
    token = lax.broadcasted_iota(jnp.int32, (token_rows, entries), 0)
    widen = (lane // top_count == token).astype(jnp.float32).astype(jnp.bfloat16)
    wide = lax.dot_general(
        ids_ref[...].astype(jnp.float32).astype(jnp.bfloat16), widen, NN, preferred_element_type=jnp.float32
    )
    choice = lax.broadcasted_iota(jnp.int32, (top_count, entries), 1) % top_count
    own_choice = choice == lax.broadcasted_iota(jnp.int32, (top_count, entries), 0)
    ids = jnp.sum(jnp.where(own_choice, wide, 0.0), axis=0, keepdims=True).astype(jnp.int32)
    onehot = lax.broadcasted_iota(jnp.int32, (devices, entries), 0) == ids
    onehot_f = onehot.astype(jnp.float32)
    onehot_b = onehot_f.astype(jnp.bfloat16)
    earlier = (
        lax.broadcasted_iota(jnp.int32, (entries, entries), 0)
        < lax.broadcasted_iota(jnp.int32, (entries, entries), 1)
    ).astype(jnp.float32).astype(jnp.bfloat16)
    before = lax.dot_general(onehot_b, earlier, NN, preferred_element_type=jnp.float32)
    rank = jnp.sum(before * onehot_f, axis=0, keepdims=True).astype(jnp.int32)
    target = ids * slots + rank
    for i in range(0, devices * slots, BLK):
        row = lax.broadcasted_iota(jnp.int32, (BLK, entries), 0) + i
        pick[i : i + BLK, :] = (row == target).astype(jnp.float32).astype(jnp.bfloat16)
    load.wait()

    def build(c):
        part = lax.dot_general(
            pick[...], part_of(c).astype(jnp.bfloat16), NN, preferred_element_type=jnp.float32
        )
        outbox[c] = part.reshape(devices, slots, BLK).astype(jnp.bfloat16)
        inbox[c, me] = outbox[c, me]

    def send(c):
        def one(offset, carry):
            peer, device = place(offset)
            pltpu.make_async_remote_copy(
                src_ref=outbox.at[c, peer],
                dst_ref=inbox.at[c, me],
                send_sem=send_sem.at[c],
                recv_sem=recv_sem.at[c],
                device_id=device,
                device_id_type=pl.DeviceIdType.MESH,
            ).start()
            return carry

        lax.fori_loop(1, devices, one, 0)

    def send_stats(offset, carry):
        peer, device = place(offset)
        pltpu.make_async_remote_copy(
            src_ref=stat_out.at[peer],
            dst_ref=stat_in.at[me],
            send_sem=stat_sem.at[0],
            recv_sem=stat_sem.at[1],
            device_id=device,
            device_id_type=pl.DeviceIdType.MESH,
        ).start()
        return carry

    build(0)
    pl.semaphore_wait(barrier, devices - 1)
    send(0)
    build(1)
    counts = jnp.sum(onehot_f, axis=1, keepdims=True)
    squares = jnp.zeros((devices, BLK), jnp.float32)
    for c in range(steps):
        v = part_of(c)
        hi, lo = split(v * v)
        squares = squares + lax.dot_general(onehot_b, hi, NN, preferred_element_type=jnp.float32)
        squares = squares + lax.dot_general(onehot_b, lo, NN, preferred_element_type=jnp.float32)
    squares = jnp.sum(squares, axis=1, keepdims=True)
    first = lax.broadcasted_iota(jnp.int32, (devices, BLK), 1) < BLK // 2
    stats = jnp.where(first, jnp.broadcast_to(counts, (devices, BLK)), jnp.broadcast_to(squares, (devices, BLK)))
    for d in range(devices):
        stat_out[d] = stats[d : d + 1, :]
    stat_in[me] = stat_out[me]

    for c in range(2, min(3, steps)):
        build(c)
    lax.fori_loop(1, devices, send_stats, 0)
    for c in range(1, min(WINDOW, steps)):
        send(c)
    for c in range(3, steps):
        build(c)
    o_ref[...] = jnp.zeros_like(o_ref)
    wh[...] = jnp.zeros_like(wh)
    wl[...] = jnp.zeros_like(wl)

    def settle(ref, sem):
        part = ref.at[pl.ds(0, devices - 1)]
        pltpu.make_async_copy(part, part, sem).wait()

    settle(stat_in, stat_sem.at[1])
    total = stat_in[0]
    for d in range(1, devices):
        total = total + stat_in[d]
    spread = lambda x: jnp.broadcast_to(x, (SUB, BLK))
    inv_count = 1.0 / spread(total[:, 0:1])
    shift = damping * (spread(total[:, BLK // 2 : BLK // 2 + 1]) * inv_count / n)
    scale_ref[0] = inv_count
    scale_ref[1] = shift
    inv_count, shift = inv_count[0:1, :], shift[0:1, :]

    def take(k):
        settle(inbox.at[k], recv_sem.at[k])
        x_ref[:, pl.ds(pl.multiple_of(k * BLK, BLK), BLK)] = (
            inbox[k].reshape(devices * slots, BLK)
        )

    def step(k, carry):
        base = pl.multiple_of(k * BLK, BLK)

        @pl.when(k + WINDOW < steps)
        def _():
            send(k + WINDOW)

        take(k)
        for i in range(steps - 1):

            @pl.when(k == i)
            def _():
                s, t = whole_block(x_ref, wh, wl, i, inv_count, shift)
                s_ref[...] = s
                if i:
                    t_ref[:, : i * BLK] = t

        own = diag_inverse(s_ref[...])
        at = (pl.ds(base, BLK), pl.ds(base, BLK))
        o_ref[at] = own
        own_hi, own_lo = split(own)
        wh[at] = own_hi
        wl[at] = own_lo
        for i in range(1, steps - 1):

            @pl.when(k == i)
            def _():
                a = i * BLK
                row = -dot3((own_hi, own_lo), split(t_ref[:, :a]), NN)
                o_ref[a : a + BLK, :a] = row
                hi, lo = split(row)
                wh[a : a + BLK, :a] = hi
                wl[a : a + BLK, :a] = lo

        return carry

    lax.fori_loop(0, steps - 1, step, 0)
    settle(stat_out, stat_sem.at[0])

    def drain(c, carry):
        settle(outbox.at[c], send_sem.at[c])
        return carry

    lax.fori_loop(0, steps, drain, 0)
    take(steps - 1)


def last_kernel(o_ref, wh, wl, x_ref, scale_ref, out_ref, last, sems):
    n = x_ref.shape[1]
    done = n - BLK
    early = pltpu.make_async_copy(o_ref, out_ref.at[pl.ds(0, done)], sems.at[0])
    early.start()
    s, t = whole_block(x_ref, wh, wl, n // BLK - 1, scale_ref[0, 0:1, :], scale_ref[1, 0:1, :])
    own = diag_inverse(s)
    last[:, done:] = own
    t = split(t)
    moves = [early]
    for q, b0 in enumerate(range(0, BLK, PAN)):
        e = b0 + PAN
        part = split(own[b0:e, :e])
        last[b0:e, :done] = -dot3(part, (t[0][:e], t[1][:e]), NN)
        move = pltpu.make_async_copy(last.at[pl.ds(b0, PAN)], out_ref.at[pl.ds(done + b0, PAN)], sems.at[1 + q])
        move.start()
        moves.append(move)
    for move in moves:
        move.wait()


def shards(captured, expert_ids):
    devices = lax.axis_size("tok") * lax.axis_size("exp")
    token_rows, top_count, n = captured.shape
    entries = token_rows * top_count
    slots = 2 * entries // devices
    steps = n // BLK
    done = n - BLK
    vmem = pl.BlockSpec(memory_space=pltpu.VMEM)
    hbm = pl.BlockSpec(memory_space=pltpu.HBM)
    bf16, f32 = jnp.bfloat16, jnp.float32
    box = pltpu.VMEM((steps, devices, slots, BLK), bf16)
    stat = pltpu.VMEM((devices, 1, BLK), f32)
    parts = pl.pallas_call(
        exchange_kernel,
        out_shape=[
            pltpu.VMEM((done, n), f32),
            pltpu.VMEM((done, done), bf16),
            pltpu.VMEM((done, done), bf16),
            pltpu.VMEM((devices * slots, n), bf16),
            pltpu.VMEM((2, SUB, BLK), f32),
        ],
        in_specs=[vmem, hbm],
        out_specs=[vmem] * 5,
        scratch_shapes=[
            pltpu.VMEM((token_rows, top_count, n), bf16),
            pltpu.VMEM((BLK, BLK), f32),
            pltpu.VMEM((BLK, n), f32),
            pltpu.VMEM((devices * slots, entries), bf16),
            box,
            box,
            stat,
            stat,
            pltpu.SemaphoreType.DMA,
            pltpu.SemaphoreType.DMA((steps,)),
            pltpu.SemaphoreType.DMA((steps,)),
            pltpu.SemaphoreType.DMA((2,)),
        ],
        compiler_params=pltpu.CompilerParams(collective_id=0, has_side_effects=True, vmem_limit_bytes=50 << 20),
        name="exchange_whiten",
    )(expert_ids.T, captured)
    out = pl.pallas_call(
        last_kernel,
        out_shape=jax.ShapeDtypeStruct((n, n), f32),
        in_specs=[vmem] * 5,
        out_specs=pl.BlockSpec(memory_space=pl.ANY),
        scratch_shapes=[pltpu.VMEM((BLK, n), f32), pltpu.SemaphoreType.DMA((1 + BLK // PAN,))],
        compiler_params=pltpu.CompilerParams(vmem_limit_bytes=36 << 20),
        name="whiten_last",
    )(*parts)
    return out[None]


def solution(mesh):
    placed = (P(("tok", "exp"), None, None), P(("tok", "exp"), None))
    return jax.shard_map(
        shards, mesh=mesh, in_specs=placed, out_specs=P(("tok", "exp"), None, None), check_vma=False
    )
```

```python
import jax
import jax.numpy as jnp
from jax import lax
from jax.experimental import pallas as pl
from jax.experimental.pallas import tpu as pltpu
from jax.sharding import PartitionSpec as P

damping = 0.1
BLK = 128
SUB = 8
PAN = 32
WINDOW = 2

NN = (((1,), (0,)), ((), ()))
NT = (((1,), (1,)), ((), ()))
TN = (((0,), (0,)), ((), ()))


def split(a):
    hi = a.astype(jnp.bfloat16)
    lo = (a - hi.astype(jnp.float32)).astype(jnp.bfloat16)
    return hi, lo


def dot3(a, b, dims):
    ah, al = a
    bh, bl = b
    d = lambda x, y: lax.dot_general(x, y, dims, preferred_element_type=jnp.float32)
    rows = ah.shape[0]
    both = d(jnp.concatenate([ah, al], axis=0), bh)
    return both[:rows] + (d(ah, bl) + both[rows:])


def diag_inverse(full):
    n = full.shape[0]
    size = min(PAN, n)
    count = size // SUB
    sub = lax.broadcasted_iota(jnp.int32, (SUB, n), 0)
    lane = lax.broadcasted_iota(jnp.int32, (SUB, n), 1)
    zero = (sub * 0).astype(jnp.float32)
    spread = lambda x: jnp.broadcast_to(x, (SUB, n))
    columns = lambda v, c: [spread(v[:, c + t : c + t + 1]) + zero for t in range(SUB)]
    out = []
    for b0 in range(0, n, size):
        rows = [full[SUB * r : SUB * (r + 1), :] for r in range(count)]
        own = columns(rows[0], b0)
        side = columns(rows[1], b0)
        after = columns(rows[1], b0 + SUB)
        for p in range(count):
            c0 = b0 + SUB * p
            more = p + 1 < count
            inside = (lane >= c0) & (lane < c0 + SUB)
            row = jnp.where(inside, jnp.where(lane - c0 == sub, 1.0, 0.0), rows[p])
            below = jnp.where(inside, 0.0, rows[p + 1]) if more else None
            tops, invs, heads = [], [], []
            pivots = None
            for s in range(SUB):
                top = {t: spread(own[s][t : t + 1, :]) for t in range(s, SUB)}
                inv = 1.0 / top[s]
                pivots = jnp.where(sub >= s, top[s], pivots) if s else top[s]
                head = spread(row[s : s + 1, :])
                if s < SUB - 1:
                    m = jnp.where(sub > s, own[s] * inv, 0.0)
                    for t in range(s + 1, SUB):
                        own[t] = own[t] - m * top[t]
                    row = row - m * head
                if more:
                    x = side[s]
                    m = x * inv
                    for t in range(s + 1, SUB):
                        side[t] = side[t] - m * top[t]
                    below = below - m * head
                    for t in range(SUB):
                        after[t] = after[t] - m * spread(x[t : t + 1, :])
                tops.append(top)
                invs.append(inv)
                heads.append(head)
            rows[p] = row * lax.rsqrt(pivots)
            if more:
                rows[p + 1] = below
            own = after
            if p + 2 < count:
                solved = [None] * SUB
                for t in range(SUB - 1, -1, -1):
                    v = heads[t]
                    for k in range(SUB - 1, t, -1):
                        v = v - tops[t][k] * solved[k]
                    solved[t] = v * invs[t]
                for r in range(p + 2, count):
                    acc = jnp.where(inside, 0.0, rows[r])
                    for col, v in zip(columns(rows[r], c0), solved):
                        acc = acc - col * v
                    rows[r] = acc
                side = columns(rows[p + 2], c0 + SUB)
                after = columns(rows[p + 2], c0 + 2 * SUB)
        lower = [jnp.where(lane <= b0 + SUB * p + sub, rows[p], 0.0) for p in range(count)]
        out += lower
        if b0 + size < n:
            both = jnp.concatenate(
                [jnp.where(lane >= b0 + size, rows[p], lower[p]) for p in range(count)], axis=0
            )
            hi, lo = split(both)
            update = lax.dot_general(
                jnp.concatenate([hi, hi, lo], axis=0),
                jnp.concatenate([hi, lo, hi], axis=0),
                TN,
                preferred_element_type=jnp.float32,
            )
            rest = full[size:, :]
            spot = lax.broadcasted_iota(jnp.int32, rest.shape, 1)
            full = jnp.where((spot >= b0) & (spot < b0 + size), 0.0, rest) - update[b0 + size :, :]
    return jnp.concatenate(out, axis=0)


def whole_block(x_ref, wh, wl, i, inv_count, shift):
    a = i * BLK
    eye = (
        lax.broadcasted_iota(jnp.int32, (BLK, BLK), 0) == lax.broadcasted_iota(jnp.int32, (BLK, BLK), 1)
    ).astype(jnp.float32)
    gram = lax.dot_general(x_ref[:, a : a + BLK], x_ref[:, : a + BLK], TN, preferred_element_type=jnp.float32)
    s = gram[:, a:] * inv_count + shift * eye
    if not i:
        return s, None
    g_hi, g_lo = split(gram[:, :a] * inv_count[:, 0:1])
    cuts = [(j, min(j + 2 * BLK, a)) for j in range(0, a, 2 * BLK)]
    low = jnp.concatenate(
        [dot3((g_hi[:, :e], g_lo[:, :e]), (wh[j:e, :e], wl[j:e, :e]), NT) for j, e in cuts], axis=1
    )
    l_hi, l_lo = split(low)
    s = s - dot3((l_hi, l_lo), (l_hi, l_lo), NT)
    t = jnp.concatenate(
        [dot3((l_hi[:, j:], l_lo[:, j:]), (wh[j:a, j:e], wl[j:a, j:e]), NN) for j, e in cuts], axis=1
    )
    return s, t


def exchange_kernel(
    ids_ref, in_hbm, o_ref, wh, wl, x_ref, scale_ref, in_ref, s_ref, t_ref, pick, outbox, inbox, stat_out, stat_in,
    in_sem, send_sem, recv_sem, stat_sem,
):
    n = x_ref.shape[1]
    steps = n // BLK
    _, devices, slots, _ = outbox.shape
    top_count, token_rows = ids_ref.shape
    entries = token_rows * top_count
    exp_size = lax.axis_size("exp")
    me = lax.axis_index("tok") * exp_size + lax.axis_index("exp")

    def place(offset):
        peer = lax.rem(me + offset, devices)
        return peer, (peer // exp_size, lax.rem(peer, exp_size))

    def part_of(c):
        part = in_ref[:, :, c * BLK : (c + 1) * BLK].astype(jnp.float32)
        return part.reshape(entries, BLK)

    barrier = pltpu.get_barrier_semaphore()

    def greet(offset, carry):
        pl.semaphore_signal(barrier, inc=1, device_id=place(offset)[1], device_id_type=pl.DeviceIdType.MESH)
        return carry

    loads = []
    for i, at in enumerate((pl.ds(0, BLK), pl.ds(BLK, n - BLK))):
        loads.append(pltpu.make_async_copy(in_hbm.at[:, :, at], in_ref.at[:, :, at], in_sem.at[i]))
        loads[i].start()
    def far_first(step, carry):
        exp, tok = lax.axis_index("exp"), lax.axis_index("tok")
        toks = devices // exp_size
        j = step // toks
        peer_exp = lax.select(exp >= exp_size // 2, j, exp_size - 1 - j)
        peer_tok = lax.rem(toks - 1 - tok + lax.rem(step, toks), toks)

        @pl.when((peer_exp != exp) | (peer_tok != tok))
        def _():
            pl.semaphore_signal(barrier, inc=1, device_id=(peer_tok, peer_exp), device_id_type=pl.DeviceIdType.MESH)

        return carry

    lax.fori_loop(0, devices, far_first, 0)

    lane = lax.broadcasted_iota(jnp.int32, (token_rows, entries), 1)
    token = lax.broadcasted_iota(jnp.int32, (token_rows, entries), 0)
    widen = (lane // top_count == token).astype(jnp.float32).astype(jnp.bfloat16)
    wide = lax.dot_general(
        ids_ref[...].astype(jnp.float32).astype(jnp.bfloat16), widen, NN, preferred_element_type=jnp.float32
    )
    choice = lax.broadcasted_iota(jnp.int32, (top_count, entries), 1) % top_count
    own_choice = choice == lax.broadcasted_iota(jnp.int32, (top_count, entries), 0)
    ids = jnp.sum(jnp.where(own_choice, wide, 0.0), axis=0, keepdims=True).astype(jnp.int32)
    onehot = lax.broadcasted_iota(jnp.int32, (devices, entries), 0) == ids
    onehot_f = onehot.astype(jnp.float32)
    onehot_b = onehot_f.astype(jnp.bfloat16)
    earlier = (
        lax.broadcasted_iota(jnp.int32, (entries, entries), 0)
        < lax.broadcasted_iota(jnp.int32, (entries, entries), 1)
    ).astype(jnp.float32).astype(jnp.bfloat16)
    before = lax.dot_general(onehot_b, earlier, NN, preferred_element_type=jnp.float32)
    rank = jnp.sum(before * onehot_f, axis=0, keepdims=True).astype(jnp.int32)
    target = ids * slots + rank
    for i in range(0, devices * slots, BLK):
        row = lax.broadcasted_iota(jnp.int32, (BLK, entries), 0) + i
        pick[i : i + BLK, :] = (row == target).astype(jnp.float32).astype(jnp.bfloat16)
    loads[0].wait()

    def build(c):
        part = lax.dot_general(
            pick[...], part_of(c).astype(jnp.bfloat16), NN, preferred_element_type=jnp.float32
        )
        outbox[c] = part.reshape(devices, slots, BLK).astype(jnp.bfloat16)
        inbox[c, me] = outbox[c, me]

    def send(c):
        def one(offset, carry):
            peer, device = place(offset)
            pltpu.make_async_remote_copy(
                src_ref=outbox.at[c, peer],
                dst_ref=inbox.at[c, me],
                send_sem=send_sem.at[c],
                recv_sem=recv_sem.at[c],
                device_id=device,
                device_id_type=pl.DeviceIdType.MESH,
            ).start()
            return carry

        lax.fori_loop(1, devices, one, 0)

    def send_stats(offset, carry):
        peer, device = place(offset)
        pltpu.make_async_remote_copy(
            src_ref=stat_out.at[peer],
            dst_ref=stat_in.at[me],
            send_sem=stat_sem.at[0],
            recv_sem=stat_sem.at[1],
            device_id=device,
            device_id_type=pl.DeviceIdType.MESH,
        ).start()
        return carry

    build(0)
    pl.semaphore_wait(barrier, devices - 1)
    send(0)
    loads[1].wait()
    build(1)
    counts = jnp.sum(onehot_f, axis=1, keepdims=True)
    squares = jnp.zeros((devices, BLK), jnp.float32)
    for c in range(steps):
        v = part_of(c)
        hi, lo = split(v * v)
        squares = squares + lax.dot_general(onehot_b, hi, NN, preferred_element_type=jnp.float32)
        squares = squares + lax.dot_general(onehot_b, lo, NN, preferred_element_type=jnp.float32)
    squares = jnp.sum(squares, axis=1, keepdims=True)
    first = lax.broadcasted_iota(jnp.int32, (devices, BLK), 1) < BLK // 2
    stats = jnp.where(first, jnp.broadcast_to(counts, (devices, BLK)), jnp.broadcast_to(squares, (devices, BLK)))
    for d in range(devices):
        stat_out[d] = stats[d : d + 1, :]
    stat_in[me] = stat_out[me]

    for c in range(2, min(3, steps)):
        build(c)
    lax.fori_loop(1, devices, send_stats, 0)
    for c in range(1, min(WINDOW, steps)):
        send(c)
    for c in range(3, steps):
        build(c)
    o_ref[...] = jnp.zeros_like(o_ref)
    wh[...] = jnp.zeros_like(wh)
    wl[...] = jnp.zeros_like(wl)

    def settle(ref, sem):
        part = ref.at[pl.ds(0, devices - 1)]
        pltpu.make_async_copy(part, part, sem).wait()

    settle(stat_in, stat_sem.at[1])
    total = stat_in[0]
    for d in range(1, devices):
        total = total + stat_in[d]
    spread = lambda x: jnp.broadcast_to(x, (SUB, BLK))
    inv_count = 1.0 / spread(total[:, 0:1])
    shift = damping * (spread(total[:, BLK // 2 : BLK // 2 + 1]) * inv_count / n)
    scale_ref[0] = inv_count
    scale_ref[1] = shift
    inv_count, shift = inv_count[0:1, :], shift[0:1, :]

    def take(k):
        settle(inbox.at[k], recv_sem.at[k])
        x_ref[:, pl.ds(pl.multiple_of(k * BLK, BLK), BLK)] = (
            inbox[k].reshape(devices * slots, BLK)
        )

    def step(k, carry):
        base = pl.multiple_of(k * BLK, BLK)

        @pl.when(k + WINDOW < steps)
        def _():
            send(k + WINDOW)

        take(k)
        for i in range(steps - 1):

            @pl.when(k == i)
            def _():
                s, t = whole_block(x_ref, wh, wl, i, inv_count, shift)
                s_ref[...] = s
                if i:
                    t_ref[:, : i * BLK] = t

        own = diag_inverse(s_ref[...])
        at = (pl.ds(base, BLK), pl.ds(base, BLK))
        o_ref[at] = own
        own_hi, own_lo = split(own)
        wh[at] = own_hi
        wl[at] = own_lo
        for i in range(1, steps - 1):

            @pl.when(k == i)
            def _():
                a = i * BLK
                row = -dot3((own_hi, own_lo), split(t_ref[:, :a]), NN)
                o_ref[a : a + BLK, :a] = row
                hi, lo = split(row)
                wh[a : a + BLK, :a] = hi
                wl[a : a + BLK, :a] = lo

        return carry

    lax.fori_loop(0, steps - 1, step, 0)
    settle(stat_out, stat_sem.at[0])

    def drain(c, carry):
        settle(outbox.at[c], send_sem.at[c])
        return carry

    lax.fori_loop(0, steps, drain, 0)
    take(steps - 1)


def last_kernel(o_ref, wh, wl, x_ref, scale_ref, out_ref, last, sems):
    n = x_ref.shape[1]
    done = n - BLK
    early = pltpu.make_async_copy(o_ref, out_ref.at[pl.ds(0, done)], sems.at[0])
    early.start()
    s, t = whole_block(x_ref, wh, wl, n // BLK - 1, scale_ref[0, 0:1, :], scale_ref[1, 0:1, :])
    own = diag_inverse(s)
    last[:, done:] = own
    t = split(t)
    moves = [early]
    for q, b0 in enumerate(range(0, BLK, PAN)):
        e = b0 + PAN
        part = split(own[b0:e, :e])
        last[b0:e, :done] = -dot3(part, (t[0][:e], t[1][:e]), NN)
        move = pltpu.make_async_copy(last.at[pl.ds(b0, PAN)], out_ref.at[pl.ds(done + b0, PAN)], sems.at[1 + q])
        move.start()
        moves.append(move)
    for move in moves:
        move.wait()


def shards(captured, expert_ids):
    devices = lax.axis_size("tok") * lax.axis_size("exp")
    token_rows, top_count, n = captured.shape
    entries = token_rows * top_count
    slots = 2 * entries // devices
    steps = n // BLK
    done = n - BLK
    vmem = pl.BlockSpec(memory_space=pltpu.VMEM)
    hbm = pl.BlockSpec(memory_space=pltpu.HBM)
    bf16, f32 = jnp.bfloat16, jnp.float32
    box = pltpu.VMEM((steps, devices, slots, BLK), bf16)
    stat = pltpu.VMEM((devices, 1, BLK), f32)
    parts = pl.pallas_call(
        exchange_kernel,
        out_shape=[
            pltpu.VMEM((done, n), f32),
            pltpu.VMEM((done, done), bf16),
            pltpu.VMEM((done, done), bf16),
            pltpu.VMEM((devices * slots, n), bf16),
            pltpu.VMEM((2, SUB, BLK), f32),
        ],
        in_specs=[vmem, hbm],
        out_specs=[vmem] * 5,
        scratch_shapes=[
            pltpu.VMEM((token_rows, top_count, n), bf16),
            pltpu.VMEM((BLK, BLK), f32),
            pltpu.VMEM((BLK, n), f32),
            pltpu.VMEM((devices * slots, entries), bf16),
            box,
            box,
            stat,
            stat,
            pltpu.SemaphoreType.DMA((2,)),
            pltpu.SemaphoreType.DMA((steps,)),
            pltpu.SemaphoreType.DMA((steps,)),
            pltpu.SemaphoreType.DMA((2,)),
        ],
        compiler_params=pltpu.CompilerParams(collective_id=0, has_side_effects=True, vmem_limit_bytes=50 << 20),
        name="exchange_whiten",
    )(expert_ids.T, captured)
    out = pl.pallas_call(
        last_kernel,
        out_shape=jax.ShapeDtypeStruct((n, n), f32),
        in_specs=[vmem] * 5,
        out_specs=pl.BlockSpec(memory_space=pl.ANY),
        scratch_shapes=[pltpu.VMEM((BLK, n), f32), pltpu.SemaphoreType.DMA((1 + BLK // PAN,))],
        compiler_params=pltpu.CompilerParams(vmem_limit_bytes=36 << 20),
        name="whiten_last",
    )(*parts)
    return out[None]


def solution(mesh):
    placed = (P(("tok", "exp"), None, None), P(("tok", "exp"), None))
    return jax.shard_map(
        shards, mesh=mesh, in_specs=placed, out_specs=P(("tok", "exp"), None, None), check_vma=False
    )
```
